128 devices in a mesh: ens: 4 (over z_lo, core), grid: 32 (over z_hi, y, x).
Axes of the slice: x: 4, y: 4, z: 4 (z_hi: 2, z_lo: 2; z = z_hi * 2 + z_lo), core: 2. Of those that a mesh axis runs over, the one named last changes fastest.
Arguments:
- encoded_state: bfloat16 [8, 1024, 32768], P('ens', None, 'grid'), may hold values from -6 to 6
- observed_state: float32 [80, 32768], P(None, 'grid'), may hold values from -6 to 6
- location_importance: float32 [32768], P('grid'), may hold values from 0.5 to 5
- w_in: bfloat16 [1024, 1024], replicated, may hold values from -0.1875 to 0.1875
- b_in: float32 [1024], replicated, may hold values from -3 to 3
- final_matrix: bfloat16 [80, 1024], replicated, may hold values from -0.1875 to 0.1875
Outputs:
- latent_sensitivity: bfloat16 [8, 1024, 32768], P('ens', None, 'grid')
- grad_w_in: float32 [1024, 1024], P('grid')
- grad_w_out: float32 [80, 1024], replicated
- grad_b_in: float32 [1024], replicated
The draws below stay inside these ranges and needn't reach their ends.
All inputs are finite; a program needn't handle non-finite values.
Results may differ from the reference program's by a relative error of at most 0.0025.
The reference program's roundings to bfloat16 on the way count: a program that leaves them out, or rounds other values in their place, can miss the bound.
Values sent between devices are 32-bit elements; how exact they have to be, the bound alone decides.
No kernel may reach another device: no remote copies, remote signals or barrier semaphores. Data moves between devices by JAX's collectives and lax.ppermute only.
A program may use at most 128 MiB of HBM per device.

```python
import math
import jax
import jax.numpy as jnp
from jax import lax

DL = 1024
H = 1024
C = 80
E = 8
G = 32768


def block_levels(stream_key, shape, shards, low, top_value):
    gain = 1.0
    for position, blocks in shards:
        steps = jax.random.uniform(jax.random.fold_in(jax.random.fold_in(stream_key, 6), position), (blocks,), jnp.float32, low / len(shards), top_value / len(shards))
        gain = gain * jnp.repeat(jnp.exp(steps), shape[position] // blocks).reshape((-1,) + (1,) * (len(shape) - 1 - position))
    return gain


def gaussian(stream_key, extent, deviation, bound, pieces=(), dtype=jnp.bfloat16):
    entries = deviation * jax.random.normal(stream_key, extent, jnp.float32)
    if pieces:
        entries = entries * block_levels(stream_key, extent, pieces, -0.22, 0.18)
    return jnp.clip(entries, -bound, bound).astype(dtype)


def setup_inputs(seed: int = 0) -> dict:
    key_list = jax.random.split(jax.random.key(seed), 7)
    return {
        "encoded_state": gaussian(key_list[0], (E, DL, G), 1.0, 6.0, ((0, 4), (2, 32))),
        "observed_state": gaussian(key_list[1], (C, G), 1.0, 6.0, ((1, 32),), jnp.float32),
        "location_importance": jnp.clip(jnp.exp(math.log(5.0) - 2.3025851 * jax.random.uniform(key_list[2], (G,), jnp.float32) ** block_levels(key_list[2], (G,), ((0, 32),), -0.2, 0.2)), 0.5, 5.0),
        "w_in": gaussian(key_list[3], (H, DL), DL ** -0.5, 0.1875),
        "b_in": gaussian(key_list[4], (H,), 0.5, 3.0, (), jnp.float32),
        "final_matrix": gaussian(key_list[5], (C, H), H ** -0.5, 0.1875),
    }


delta_abs = 0.1
fair_alpha = 0.95

def smooth_sign_derivative(diff):
    return diff / jnp.sqrt(diff * diff + delta_abs * delta_abs)

def gelu_tanh(value):
    return jax.nn.gelu(value, approximate=True)

def reference(encoded_state, observed_state, location_importance, w_in, b_in, final_matrix):
    members = encoded_state.shape[0]
    points = encoded_state.shape[2]

    def layer_one(member_latent):
        pre_act = jnp.dot(w_in, member_latent, preferred_element_type=jnp.float32) + b_in[:, None]
        inner_response = gelu_tanh(pre_act).astype(jnp.bfloat16)
        return (pre_act, inner_response)

    def forward_apply(member_latent):
        pre_act, inner_response = layer_one(member_latent)
        return jnp.dot(final_matrix, inner_response, preferred_element_type=jnp.float32)
    estimated_channels = lax.map(forward_apply, encoded_state)

    def pairwise_row(member_prediction):
        return lax.optimization_barrier(jnp.sum(smooth_sign_derivative(member_prediction[None] - estimated_channels), axis=0))
    couple_aggregate = lax.map(pairwise_row, estimated_channels)
    couple_multiplier = (1.0 - (1.0 - fair_alpha) / members) / (members - 1)
    ensemble_sensitivity = (location_importance[None, None, :] * (smooth_sign_derivative(estimated_channels - observed_state[None]) - couple_multiplier * couple_aggregate)).astype(jnp.bfloat16)

    def reverse_sweep(totals, inputs):
        member_latent, member_grad = inputs
        pre_act, inner_response = layer_one(member_latent)
        back_hidden = jnp.dot(final_matrix.T, member_grad, preferred_element_type=jnp.float32)
        _, pull = jax.vjp(gelu_tanh, pre_act)
        grad_pre = pull(back_hidden)[0].astype(jnp.bfloat16)
        grad_member = jnp.dot(w_in.T, grad_pre, preferred_element_type=jnp.float32).astype(jnp.bfloat16)
        in_sum = totals[0] + jnp.dot(grad_pre, member_latent.T, preferred_element_type=jnp.float32)
        out_sum = totals[1] + jnp.dot(member_grad, inner_response.T, preferred_element_type=jnp.float32)
        bias_sum = totals[2] + lax.optimization_barrier(jnp.sum(grad_pre.astype(jnp.float32), axis=1))
        return ((in_sum, out_sum, bias_sum), grad_member)
    starting_parameters = (jnp.zeros(w_in.shape, jnp.float32), jnp.zeros(final_matrix.shape, jnp.float32), jnp.zeros(b_in.shape, jnp.float32))
    accumulated_parts, latent_sensitivity = lax.scan(reverse_sweep, starting_parameters, (encoded_state, ensemble_sensitivity))
    grad_scale = 1.0 / math.sqrt(members * points)
    return (latent_sensitivity, accumulated_parts[0] * grad_scale, accumulated_parts[1] * grad_scale, accumulated_parts[2] * grad_scale)
```

```python
import math

import numpy as np
import jax
import jax.numpy as jnp
from jax import lax
from jax.sharding import PartitionSpec as P

delta_abs = 0.1
fair_alpha = 0.95
AXES = ("ens", "grid")


def decode(index):
    e, g = divmod(index, 32)
    zl, c = divmod(e, 2)
    zh, r = divmod(g, 16)
    y, x = divmod(r, 4)
    return x, y, zh * 2 + zl, c


def encode(x, y, z, c):
    return ((z % 2) * 2 + c) * 32 + (z // 2) * 16 + y * 4 + x


HIGH = ((0, 1, 1, 0), (0, 0, 1, 1))
LOW = ((0, 0, 1, 1), (0, 1, 1, 0))


def cubes(stage):
    found = {}
    for index in range(128):
        x, y, z, c = decode(index)
        digit, other = (HIGH[c], LOW[c]) if stage == 0 else (LOW[c], HIGH[c])
        place = (digit[x], digit[y], digit[z])
        found.setdefault((c, other[x], other[y], other[z]), []).append((place, index))
    return [[index for _, index in sorted(v)] for _, v in sorted(found.items())]


CUBES = (cubes(0), cubes(1))
SWAP_CORE = [(i, encode(*decode(i)[:3], 1 - decode(i)[3])) for i in range(128)]
SWAP_Z = [(i, encode(decode(i)[0], decode(i)[1], decode(i)[2] ^ 1, decode(i)[3])) for i in range(128)]


def block_order(c):
    coordinate = {(HIGH[c][u], LOW[c][u]): u for u in range(4)}
    order = []
    for place in range(64):
        kx1, ky1, kz1, kx2, ky2, last = ((place >> s) & 1 for s in (5, 4, 3, 2, 1, 0))
        x, y = coordinate[kx1, kx2], coordinate[ky1, ky2]
        zh, half = (last, kz1) if c == 0 else (kz1, last)
        order.append(((zh * 4 + y) * 4 + x) * 2 + half)
    return order


ORDER = np.array([block_order(0), block_order(1)], np.int32)


def all_to_all(value, groups):
    return lax.all_to_all(value, AXES, 0, 0, axis_index_groups=groups, tiled=True)


def reduce_all(mine, theirs, small_mine, small_theirs, core):
    x = lax.axis_index("grid") % 4
    y = (lax.axis_index("grid") // 4) % 4
    got, small_got = lax.ppermute((theirs, small_theirs), AXES, SWAP_CORE)
    blocks = (mine + got).reshape(64, 16, 512)[jnp.asarray(ORDER)[core]].reshape(8, 128, 512)
    small = (small_mine + small_got).reshape(8, 16, 512)
    first = jnp.sum(all_to_all(jnp.concatenate([blocks, small], 1), CUBES[0]), 0)
    rows = first[:128]
    small = first[128:]
    split = jnp.broadcast_to(rows.reshape(8, 1, 16, 512), (8, 2, 16, 512)).reshape(8, 32, 512)
    kept = jnp.broadcast_to(rows.reshape(4, 1, 32, 512), (4, 2, 32, 512)).reshape(8, 32, 512)
    send = jnp.concatenate(
        [jnp.where(core == 0, split, kept), jnp.broadcast_to(small[None], (8, 16, 512))], 1
    )
    second = jnp.sum(all_to_all(send, CUBES[1]), 0)
    send = jnp.concatenate([second[32:], second[:16]], 0)
    third = all_to_all(jnp.broadcast_to(send[None], (8, 32, 512)), CUBES[0])
    digits = jnp.asarray(np.array(HIGH[0], np.int32))
    pair = lax.dynamic_slice_in_dim(third[:, 16:], 2 * (digits[x] * 2 + digits[y]), 2, 0).reshape(32, 512)
    done = jnp.concatenate([jnp.where(core == 0, pair, second[:32]), third[:, :16].reshape(128, 512)], 0)
    other = lax.ppermute(done, AXES, SWAP_CORE)
    whole = jnp.where(core == 0, jnp.concatenate([done, other], 1), jnp.concatenate([other, done], 1))
    return whole[:32], whole[32:]


def smooth_sign_derivative(diff):
    return diff * lax.rsqrt(diff * diff + delta_abs * delta_abs)


def gelu_tanh(value):
    return jax.nn.gelu(value, approximate=True)


def shards(encoded_state, observed_state, location_importance, w_in, b_in, final_matrix):
    members = encoded_state.shape[0] * lax.axis_size("ens")
    points = encoded_state.shape[2] * lax.axis_size("grid")
    core = lax.axis_index("ens") % 2
    pre_act = (
        jnp.einsum("hd,mdg->mhg", w_in, encoded_state, preferred_element_type=jnp.float32)
        + b_in[None, :, None]
    )
    inner_response = gelu_tanh(pre_act).astype(jnp.bfloat16)
    forecast = jnp.einsum(
        "oe,kez->koz", final_matrix, inner_response, preferred_element_type=jnp.float32
    )
    across = lax.ppermute(forecast, AXES, SWAP_Z)
    beside = lax.ppermute(forecast, AXES, SWAP_CORE)
    diagonal = lax.ppermute(across, AXES, SWAP_CORE)
    everyone = jnp.concatenate([forecast, beside, across, diagonal], 0)
    couple_aggregate = jnp.sum(smooth_sign_derivative(forecast[:, None] - everyone[None]), axis=1)
    couple_multiplier = (1.0 - (1.0 - fair_alpha) / members) / (members - 1)
    grad_fc = (
        location_importance[None, None, :]
        * (smooth_sign_derivative(forecast - observed_state[None]) - couple_multiplier * couple_aggregate)
    ).astype(jnp.bfloat16)
    back_hidden = jnp.einsum("lv,tlj->tvj", final_matrix, grad_fc, preferred_element_type=jnp.float32)
    _, pull = jax.vjp(gelu_tanh, pre_act)
    grad_pre = pull(back_hidden)[0].astype(jnp.bfloat16)
    columns = encoded_state.shape[1] // 2

    def part(which):
        state = lax.dynamic_slice_in_dim(encoded_state, which * columns, columns, 1)
        return jnp.einsum("mhg,mdg->hd", grad_pre, state, preferred_element_type=jnp.float32)

    out_term = jnp.einsum("rbf,rwf->bw", grad_fc, inner_response, preferred_element_type=jnp.float32)
    bias_term = jnp.sum(grad_pre.astype(jnp.float32), axis=(0, 2))
    small = jnp.concatenate([out_term, bias_term[None], jnp.zeros((47, 1024), jnp.float32)], 0)

    def small_part(which):
        return lax.dynamic_slice_in_dim(small, which * columns, columns, 1)

    in_sum, small_sum = reduce_all(
        part(core), part(1 - core), small_part(core), small_part(1 - core), core
    )
    latent_sensitivity = jnp.einsum(
        "hd,mhg->mdg", w_in, grad_pre, preferred_element_type=jnp.float32
    ).astype(jnp.bfloat16)
    grad_scale = 1.0 / math.sqrt(members * points)
    return (
        latent_sensitivity,
        in_sum * grad_scale,
        small_sum[:80] * grad_scale,
        small_sum[80] * grad_scale,
    )


def solution(mesh):
    placed = (P("ens", None, "grid"), P(None, "grid"), P("grid"), P(), P(), P())
    return jax.shard_map(
        shards,
        mesh=mesh,
        in_specs=placed,
        out_specs=(P("ens", None, "grid"), P("grid", None), P(), P()),
        check_vma=False,
    )
```

```python
import functools
import math

import numpy as np
import jax
import jax.numpy as jnp
from jax import lax
from jax.experimental import pallas as pl
from jax.experimental.pallas import tpu as pltpu
from jax.sharding import PartitionSpec as P

delta_abs = 0.1
fair_alpha = 0.95
AXES = ("ens", "grid")
F32, BF16 = jnp.float32, jnp.bfloat16
HALVES = 2
ROOT = math.sqrt(2.0 / math.pi)
CUBIC = 0.044715
CHUNK = 512


def decode(index):
    e, g = divmod(index, 32)
    zl, c = divmod(e, 2)
    zh, r = divmod(g, 16)
    y, x = divmod(r, 4)
    return x, y, zh * 2 + zl, c


def encode(x, y, z, c):
    return ((z % 2) * 2 + c) * 32 + (z // 2) * 16 + y * 4 + x


SWAP_CORE = [(i, encode(*decode(i)[:3], 1 - decode(i)[3])) for i in range(128)]
SWAP_Z = [(i, encode(decode(i)[0], decode(i)[1], decode(i)[2] ^ 1, decode(i)[3])) for i in range(128)]
CHIPS = [
    [encode(x, y, 2 * zh + zl, c) for zh in (0, 1) for y in range(4) for x in range(4) for zl in (0, 1)]
    for c in (0, 1)
]


def all_to_all(value, groups):
    return lax.all_to_all(value, AXES, 0, 0, axis_index_groups=groups, tiled=True)


def dot(a, b):
    return jnp.dot(a, b, preferred_element_type=F32)


def dot_nt(a, b):
    return lax.dot_general(a, b, (((1,), (1,)), ((), ())), preferred_element_type=F32)


def params(vmem=24 << 20):
    return pltpu.CompilerParams(vmem_limit_bytes=vmem)


def cost(flops, bytes_accessed):
    return pl.CostEstimate(flops=flops, bytes_accessed=bytes_accessed, transcendentals=0)


def forward_kernel(x_ref, w_ref, b_ref, f_ref, hidden_ref, slope_ref, fc_ref, column_ref):
    @pl.when((pl.program_id(0) == 0) & (pl.program_id(1) == 0))
    def _():
        turned = b_ref[...].T
        for i in range(turned.shape[1]):
            column_ref[128 * i : 128 * i + 128, :] = turned[:, i : i + 1]

    x = x_ref[0]
    total = None
    for r in range(0, w_ref.shape[0], CHUNK):
        rows = pl.ds(r, CHUNK)
        v = dot(w_ref[rows, :], x) + column_ref[rows, :]
        v2 = v * v
        t = jnp.tanh(v * (ROOT * CUBIC * v2 + ROOT))
        a = 0.5 * t + 0.5
        hidden = (v * a).astype(BF16)
        hidden_ref[0, rows, :] = hidden
        slope_ref[0, rows, :] = a + (v * (1.5 * ROOT * CUBIC * v2 + 0.5 * ROOT)) * (1.0 - t * t)
        part = dot(f_ref[:, rows], hidden)
        total = part if total is None else total + part
    fc_ref[0] = total


def forward(state, w_in, bias, final_matrix, half):
    m, d, g = state.shape
    h, c = w_in.shape[0], final_matrix.shape[0]
    n = g // HALVES
    tile = 512
    steps = n // tile
    return pl.pallas_call(
        forward_kernel,
        grid=(m, steps),
        in_specs=[
            pl.BlockSpec((1, d, tile), lambda i, j: (i, 0, half * steps + j)),
            pl.BlockSpec((h, d), lambda i, j: (0, 0), pipeline_mode=pl.Buffered(1)),
            pl.BlockSpec(bias.shape, lambda i, j: (0, 0), pipeline_mode=pl.Buffered(1)),
            pl.BlockSpec((c, h), lambda i, j: (0, 0), pipeline_mode=pl.Buffered(1)),
        ],
        out_specs=[
            pl.BlockSpec((1, h, tile), lambda i, j: (i, 0, j)),
            pl.BlockSpec((1, h, tile), lambda i, j: (i, 0, j)),
            pl.BlockSpec((1, c, tile), lambda i, j: (i, 0, j)),
        ],
        out_shape=[
            jax.ShapeDtypeStruct((m, h, n), BF16),
            jax.ShapeDtypeStruct((m, h, n), F32),
            jax.ShapeDtypeStruct((m, c, n), F32),
        ],
        scratch_shapes=[pltpu.VMEM((h, 1), F32)],
        compiler_params=params(),
        cost_estimate=cost(2 * m * h * n * (d + c), m * n * (2 * d + 6 * h)),
        name=f"forward{half}",
    )(state, w_in, bias, final_matrix)


def slope_of(d):
    return d * lax.rsqrt(d * d + delta_abs * delta_abs)


def backward_kernel(factor, own_ref, a_ref, b_ref, c_ref, obs_ref, loc_ref, ft_ref, slope_ref, hidden_ref,
                    init_ref, gp_ref, small_ref, wide_ref, bias_ref):
    first = (pl.program_id(0) == 0) & (pl.program_id(1) == 0)
    last = (pl.program_id(0) == pl.num_programs(0) - 1) & (pl.program_id(1) == pl.num_programs(1) - 1)

    @pl.when(first)
    def _():
        wide_ref[...] = jnp.zeros_like(wide_ref)
        bias_ref[...] = jnp.zeros_like(bias_ref)

    own = own_ref[pl.program_id(0)]
    pairs = None
    for ref in (own_ref, a_ref, b_ref, c_ref):
        for k in range(ref.shape[0]):
            s = slope_of(own - ref[k])
            pairs = s if pairs is None else pairs + s
    grad = (loc_ref[...] * (slope_of(own - obs_ref[...]) - factor * pairs)).astype(BF16)
    channels = grad.shape[0]
    ones = jnp.ones((8, grad.shape[1]), BF16)
    for r in range(0, ft_ref.shape[0], CHUNK):
        rows = pl.ds(r, CHUNK)
        gp = (dot(ft_ref[rows, :], grad) * slope_ref[0, rows, :]).astype(BF16)
        gp_ref[0, rows, :] = gp
        wide_ref[rows, :channels] += dot_nt(hidden_ref[0, rows, :], grad)
        bias_ref[rows, :] += dot_nt(gp, ones)

    @pl.when(last)
    def _():
        small_ref[...] = init_ref[...]
        small_ref[:channels, :] += wide_ref[...].T[:channels, :]
        small_ref[channels : channels + 8, :] += bias_ref[...].T


def backward(fcs, observed, location, ft, slope, hidden, init, factor, half):
    m, h, n = hidden.shape
    c = ft.shape[1]
    tile = 512
    steps = n // tile
    fc_spec = pl.BlockSpec((m, c, tile), lambda i, j: (0, 0, j))
    big = pl.BlockSpec((1, h, tile), lambda i, j: (i, 0, j))
    small = pl.BlockSpec(init.shape, lambda i, j: (0, 0), pipeline_mode=pl.Buffered(1))
    return pl.pallas_call(
        functools.partial(backward_kernel, factor),
        grid=(m, steps),
        in_specs=[fc_spec] * 4
        + [
            pl.BlockSpec((c, tile), lambda i, j: (0, half * steps + j)),
            pl.BlockSpec((1, tile), lambda i, j: (0, half * steps + j)),
            pl.BlockSpec((h, c), lambda i, j: (0, 0), pipeline_mode=pl.Buffered(1)),
            big,
            big,
            small,
        ],
        out_specs=[big, pl.BlockSpec(init.shape, lambda i, j: (0, 0))],
        out_shape=[jax.ShapeDtypeStruct((m, h, n), BF16), jax.ShapeDtypeStruct(init.shape, F32)],
        scratch_shapes=[pltpu.VMEM((h, 128), F32), pltpu.VMEM((h, 8), F32)],
        compiler_params=params(),
        cost_estimate=cost(4 * m * h * n * 256, m * n * 8 * h),
        name=f"backward{half}",
    )(*fcs, observed, location, ft, slope, hidden, init)


def weight_kernel(which_ref, *refs):
    gps, (x_ref, out_ref) = refs[:HALVES], refs[HALVES:]
    h, n = gps[0].shape[1:]

    def products(r):
        return sum(dot_nt(gp[0, pl.ds(r, CHUNK), :], x_ref[0, :, i * n : (i + 1) * n]) for i, gp in enumerate(gps))

    @pl.when(pl.program_id(0) == 0)
    def _():
        for r in range(0, h, CHUNK):
            out_ref[pl.ds(r, CHUNK), :] = products(r)

    @pl.when(pl.program_id(0) != 0)
    def _():
        for r in range(0, h, CHUNK):
            out_ref[pl.ds(r, CHUNK), :] += products(r)


def weight_half(which, gps, state, name):
    m, d, g = state.shape
    h = gps[0].shape[1]
    return pl.pallas_call(
        weight_kernel,
        grid_spec=pltpu.PrefetchScalarGridSpec(
            num_scalar_prefetch=1,
            grid=(m,),
            in_specs=[pl.BlockSpec((1,) + gps[0].shape[1:], lambda i, w: (i, 0, 0))] * HALVES
            + [pl.BlockSpec((1, d // 2, g), lambda i, w: (i, w[0], 0))],
            out_specs=pl.BlockSpec((h, d // 2), lambda i, w: (0, 0)),
        ),
        out_shape=jax.ShapeDtypeStruct((h, d // 2), F32),
        compiler_params=params(),
        cost_estimate=cost(m * h * d * g, m * g * (2 * h + d) + 2 * h * d),
        name=name,
    )(which, *gps, state)


def blocks_kernel(mine_ref, got_ref, tile_ref, out_ref):
    total = mine_ref[...] + got_ref[...]
    for b in range(out_ref.shape[0]):
        for t in range(8):
            i, j = divmod(t, 4)
            out_ref[b, 8 * t : 8 * t + 8, :] = total[16 * b + 8 * i : 16 * b + 8 * i + 8, 128 * j : 128 * j + 128]
        out_ref[b, 64:72, :] = tile_ref[...]


def make_blocks(mine, got, tile):
    steps = 2
    part = pl.BlockSpec((1024 // steps, 512), lambda i: (i, 0))
    return pl.pallas_call(
        blocks_kernel,
        grid=(steps,),
        in_specs=[part, part, pl.BlockSpec((8, 128), lambda i: (0, 0))],
        out_specs=pl.BlockSpec((64 // steps, 72, 128), lambda i: (i, 0, 0)),
        out_shape=jax.ShapeDtypeStruct((64, 72, 128), F32),
        compiler_params=params(),
        cost_estimate=cost(1 << 19, 7 << 20),
        name="blocks",
    )(mine, got, tile)


def latent_kernel(w_ref, *refs):
    gps, out_ref = refs[:HALVES], refs[HALVES]
    n = gps[0].shape[2]
    for r in range(0, w_ref.shape[0], CHUNK):
        rows = pl.ds(r, CHUNK)
        for i, gp in enumerate(gps):
            out_ref[0, rows, i * n : (i + 1) * n] = dot(w_ref[rows, :], gp[0]).astype(BF16)


def latent(wt, gps):
    m, h, n = gps[0].shape
    d = wt.shape[0]
    return pl.pallas_call(
        latent_kernel,
        grid=(m,),
        in_specs=[pl.BlockSpec((d, h), lambda i: (0, 0), pipeline_mode=pl.Buffered(1))]
        + [pl.BlockSpec((1, h, n), lambda i: (i, 0, 0))] * HALVES,
        out_specs=pl.BlockSpec((1, d, HALVES * n), lambda i: (i, 0, 0)),
        out_shape=jax.ShapeDtypeStruct((m, d, HALVES * n), BF16),
        compiler_params=params(),
        cost_estimate=cost(2 * m * h * d * n * HALVES, 2 * m * n * HALVES * (h + d)),
        name="latent",
    )(wt, *gps)


def from_tiles(tiles, rows, columns):
    return tiles.reshape(rows // 8, columns // 128, 8, 128).transpose(0, 2, 1, 3).reshape(rows, columns)


def to_tiles(value):
    rows, columns = value.shape
    return value.reshape(rows // 8, 8, columns // 128, 128).transpose(0, 2, 1, 3).reshape(-1, 8, 128)


def shards(encoded_state, observed_state, location_importance, w_in, b_in, final_matrix):
    members = encoded_state.shape[0] * lax.axis_size("ens")
    points = encoded_state.shape[2] * lax.axis_size("grid")
    core = lax.axis_index("ens") % 2
    upper = lax.axis_index("ens") // 2
    mine = core.astype(jnp.int32).reshape(1)
    bias = b_in.reshape(-1, 128)
    location = location_importance.reshape(1, -1)
    ft = final_matrix.T
    factor = (1.0 - (1.0 - fair_alpha) / members) / (members - 1)

    hiddens, slopes, fcs = [], [], []
    for half in range(HALVES):
        hidden, slope, fc = forward(encoded_state, w_in, bias, final_matrix, half)
        across = lax.ppermute(fc, AXES, SWAP_Z)
        beside = lax.ppermute(fc, AXES, SWAP_CORE)
        diagonal = lax.ppermute(across, AXES, SWAP_CORE)
        hiddens.append(hidden)
        slopes.append(slope)
        fcs.append((fc, beside, across, diagonal))
    small = jnp.zeros((128, w_in.shape[0]), F32)
    gps = []
    for half in range(HALVES):
        gp, small = backward(
            fcs[half], observed_state, location, ft, slopes[half], hiddens[half], small, factor, half
        )
        gps.append(gp)
    tiles = all_to_all(to_tiles(small), [CHIPS[0] + CHIPS[1]])
    theirs = weight_half(1 - mine, gps, encoded_state, "theirs")
    got = lax.ppermute(theirs, AXES, SWAP_CORE)
    own = weight_half(mine, gps, encoded_state, "mine")
    blocks = make_blocks(own, got, jnp.sum(tiles, 0))
    blocks, weights = lax.optimization_barrier((blocks, w_in))
    spread = all_to_all(blocks, CHIPS)
    spread, latent_sensitivity = lax.optimization_barrier((spread, latent(weights.T, gps)))

    tiles = spread[:, 64:]
    rows = jnp.sum(spread[:, :64], 0)
    tiles_other = lax.ppermute(tiles, AXES, SWAP_CORE)
    rows_other = lax.ppermute(rows, AXES, SWAP_Z)
    block = jnp.stack([jnp.where(upper == 0, rows, rows_other), jnp.where(upper == 0, rows_other, rows)])
    block_other = lax.ppermute(block, AXES, SWAP_CORE)
    grad_scale = 1.0 / math.sqrt(members * points)

    def ordered(own, other):
        return jnp.where(core == 0, own, other) * grad_scale, jnp.where(core == 0, other, own) * grad_scale

    in_sum = jnp.concatenate(
        [from_tiles(part.reshape(-1, 8, 128), 32, 512) for part in ordered(block, block_other)], 1
    )
    small_sum = from_tiles(jnp.concatenate(ordered(tiles, tiles_other), 0)[:88], 88, 1024)
    return latent_sensitivity, in_sum, small_sum[:80], small_sum[80]


def solution(mesh):
    placed = (P("ens", None, "grid"), P(None, "grid"), P("grid"), P(), P(), P())
    return jax.shard_map(
        shards,
        mesh=mesh,
        in_specs=placed,
        out_specs=(P("ens", None, "grid"), P("grid", None), P(), P()),
        check_vma=False,
    )
```

```python
import functools
import math

import numpy as np
import jax
import jax.numpy as jnp
from jax import lax
from jax.experimental import pallas as pl
from jax.experimental.pallas import tpu as pltpu
from jax.sharding import PartitionSpec as P

delta_abs = 0.1
fair_alpha = 0.95
AXES = ("ens", "grid")
F32, BF16 = jnp.float32, jnp.bfloat16
HALVES = 2
ROOT = math.sqrt(2.0 / math.pi)
CUBIC = 0.044715
CHUNK = 512
FIRST, LATER = 50, 36


def decode(index):
    e, g = divmod(index, 32)
    zl, c = divmod(e, 2)
    zh, r = divmod(g, 16)
    y, x = divmod(r, 4)
    return x, y, zh * 2 + zl, c


def encode(x, y, z, c):
    return ((z % 2) * 2 + c) * 32 + (z // 2) * 16 + y * 4 + x


SWAP_CORE = [(i, encode(*decode(i)[:3], 1 - decode(i)[3])) for i in range(128)]
SWAP_Z = [(i, encode(decode(i)[0], decode(i)[1], decode(i)[2] ^ 1, decode(i)[3])) for i in range(128)]
HIGH = ((0, 1, 1, 0), (0, 0, 1, 1))
LOW = ((0, 0, 1, 1), (0, 1, 1, 0))


def cubes(stage):
    found = {}
    for index in range(128):
        x, y, z, c = decode(index)
        digit, other = (HIGH[c], LOW[c]) if stage == 0 else (LOW[c], HIGH[c])
        place = (digit[x], digit[y], digit[z])
        found.setdefault((c, other[x], other[y], other[z]), []).append((place, index))
    return [[index for _, index in sorted(v)] for _, v in sorted(found.items())]


CUBES = (cubes(0), cubes(1))


def block_order(c):
    coordinate = {(HIGH[c][u], LOW[c][u]): u for u in range(4)}
    order = []
    for place in range(64):
        kx1, ky1, kz1, kx2, ky2, last = ((place >> s) & 1 for s in (5, 4, 3, 2, 1, 0))
        x, y = coordinate[kx1, kx2], coordinate[ky1, ky2]
        zh, half = (last, kz1) if c == 0 else (kz1, last)
        order.append(((zh * 4 + y) * 4 + x) * 2 + half)
    return order


ORDER = (block_order(0), block_order(1))


def all_to_all(value, groups):
    return lax.all_to_all(value, AXES, 0, 0, axis_index_groups=groups, tiled=True)


def dot(a, b):
    return jnp.dot(a, b, preferred_element_type=F32)


def dot_nt(a, b):
    return lax.dot_general(a, b, (((1,), (1,)), ((), ())), preferred_element_type=F32)


def dot_tn(a, b):
    return lax.dot_general(a, b, (((0,), (0,)), ((), ())), preferred_element_type=F32)


def params(mib=60):
    return pltpu.CompilerParams(vmem_limit_bytes=mib << 20)


def cost(flops, bytes_accessed):
    return pl.CostEstimate(flops=flops, bytes_accessed=bytes_accessed, transcendentals=0)


def forward_rows(i, r, x, w_ref, column_ref, f_ref, hidden_ref, slope_ref):
    rows = pl.ds(r, CHUNK)
    v = dot(w_ref[rows, :], x) + column_ref[rows, :]
    v2 = v * v
    t = jnp.tanh(v * (ROOT * CUBIC * v2 + ROOT))
    a = 0.5 * t + 0.5
    hidden = (v * a).astype(BF16)
    hidden_ref[i, rows, :] = hidden
    slope_ref[i, rows, :] = a + (v * (1.5 * ROOT * CUBIC * v2 + 0.5 * ROOT)) * (1.0 - t * t)
    return dot(f_ref[:, rows], hidden)


def forward_kernel(half, first, x_any, w_any, b_any, f_any, hidden_ref, slope_ref, fc_ref, *refs):
    m, h, n = hidden_ref.shape
    starts = range(0, h, CHUNK)
    if first:
        w_ref, column_ref, x_ref, b_ref, f_ref, sems = refs
    else:
        w_ref, column_ref, f_ref, (x_ref, sems) = w_any, b_any, f_any, refs

    def copy(source, target, k):
        return pltpu.make_async_copy(source, target, sems.at[k])

    fetch_x = [copy(x_any.at[i, :, pl.ds(half * n, n)], x_ref.at[i], i) for i in range(m)]
    if first:
        fetch_b, fetch_f = copy(b_any, b_ref, m), copy(f_any, f_ref, m + 1)
        fetch_w = [copy(w_any.at[pl.ds(r, CHUNK)], w_ref.at[pl.ds(r, CHUNK)], m + 2 + j) for j, r in enumerate(starts)]
        for one in [fetch_b] + fetch_w[:1] + fetch_x[:1] + [fetch_f] + fetch_w[1:] + fetch_x[1:]:
            one.start()
        fetch_b.wait()
        turned = b_ref[...].T
        for i in range(turned.shape[1]):
            column_ref[128 * i : 128 * i + 128, :] = turned[:, i : i + 1]
    else:
        for one in fetch_x:
            one.start()
    for i in range(m):
        total = None
        fetch_x[i].wait()
        for j, r in enumerate(starts):
            if first and i == 0:
                fetch_w[j].wait()
                if j == 0:
                    fetch_f.wait()
            part = forward_rows(i, r, x_ref[i], w_ref, column_ref, f_ref, hidden_ref, slope_ref)
            total = part if total is None else total + part
        fc_ref[i] = total


VMEM = pl.BlockSpec(memory_space=pltpu.VMEM)
HBM = pl.BlockSpec(memory_space=pltpu.HBM)


def forward(state, w_in, bias, final_matrix, half, first):
    m, d, g = state.shape
    h, c = w_in.shape[0], final_matrix.shape[0]
    n = g // HALVES
    results = [
        jax.ShapeDtypeStruct((m, h, n), BF16),
        jax.ShapeDtypeStruct((m, h, n), F32),
        jax.ShapeDtypeStruct((m, c, n), F32),
    ]
    scratch = [pltpu.VMEM((m, d, n), BF16)]
    if first:
        results += [jax.ShapeDtypeStruct((h, d), BF16), jax.ShapeDtypeStruct((h, 1), F32)]
        scratch += [pltpu.VMEM(bias.shape, F32), pltpu.VMEM((c, h), BF16)]
    return pl.pallas_call(
        functools.partial(forward_kernel, half, first),
        in_specs=[HBM] * 4 if first else [HBM] + [VMEM] * 3,
        out_specs=[VMEM] * len(results),
        out_shape=results,
        scratch_shapes=scratch + [pltpu.SemaphoreType.DMA((m + 2 + h // CHUNK,))],
        compiler_params=params(FIRST if first else LATER),
        cost_estimate=cost(2 * m * h * n * (d + c), m * n * (2 * d + 6 * h)),
        name=f"forward{half}",
    )(state, w_in, bias, final_matrix)


def slope_of(d):
    return d * lax.rsqrt(d * d + delta_abs * delta_abs)


def backward_kernel(factor, half, own_ref, a_ref, b_ref, c_ref, obs_ref, loc_ref, f_ref, slope_ref, hidden_ref,
                    *refs):
    init, (gp_ref, small_ref, wide_ref, bias_ref) = refs[:-4], refs[-4:]
    m, channels, n = own_ref.shape
    here = slice(half * n, half * n + n)
    ones = jnp.ones((8, n), BF16)
    for i in range(m):
        own = own_ref[i]
        pairs = None
        for ref in (own_ref, a_ref, b_ref, c_ref):
            for k in range(m):
                s = slope_of(own - ref[k])
                pairs = s if pairs is None else pairs + s
        grad = (loc_ref[:, here] * (slope_of(own - obs_ref[:, here]) - factor * pairs)).astype(BF16)
        for r in range(0, f_ref.shape[1], CHUNK):
            rows = pl.ds(r, CHUNK)
            gp = (dot_tn(f_ref[:, rows], grad) * slope_ref[i, rows, :]).astype(BF16)
            gp_ref[i, rows, :] = gp
            wide = dot_nt(hidden_ref[i, rows, :], grad)
            bias = dot_nt(gp, ones)
            if i == 0:
                wide_ref[rows, :channels] = wide
                bias_ref[rows, :] = bias
            else:
                wide_ref[rows, :channels] += wide
                bias_ref[rows, :] += bias
    wide, bias = wide_ref[...].T[:channels, :], bias_ref[...].T
    if init:
        wide += init[0][:channels, :]
        bias += init[0][channels : channels + 8, :]
    small_ref[:channels, :] = wide
    small_ref[channels : channels + 8, :] = bias
    small_ref[channels + 8 :, :] = jnp.zeros_like(small_ref[channels + 8 :, :])


def backward(fcs, observed, location, final_matrix, slope, hidden, init, factor, half):
    m, h, n = hidden.shape
    operands = (*fcs, observed, location, final_matrix, slope, hidden, *init)
    return pl.pallas_call(
        functools.partial(backward_kernel, factor, half),
        in_specs=[VMEM] * len(operands),
        out_specs=[VMEM, VMEM],
        out_shape=[jax.ShapeDtypeStruct((m, h, n), BF16), jax.ShapeDtypeStruct((128, h), F32)],
        scratch_shapes=[
            pltpu.VMEM((h, 128), F32),
            pltpu.VMEM((h, 8), F32),
        ],
        compiler_params=params(16),
        cost_estimate=cost(4 * m * h * n * 256, m * n * 8 * h),
        name=f"backward{half}",
    )(*operands)


def weight_kernel(other, *refs):
    gps, (x_ref, *rest) = refs[:HALVES], refs[HALVES:]
    out_ref = rest[-1]
    m, h, n = gps[0].shape
    columns = out_ref.shape[1]
    core = lax.rem(lax.axis_index("ens"), 2)
    own = pl.ds(pl.multiple_of((1 - core if other else core) * columns, columns), columns)
    for r in range(0, h, CHUNK):
        rows = pl.ds(r, CHUNK)
        out_ref[rows, :] = sum(
            dot_nt(gp[i, rows, :], x_ref[i, own, k * n : (k + 1) * n]) for i in range(m) for k, gp in enumerate(gps)
        )
    if other:
        out_ref[h:, :] = rest[0][:, own]


def weight_half(gps, state, *small):
    m, d, g = state.shape
    h = gps[0].shape[1]
    rows = h + sum(one.shape[0] for one in small)
    return pl.pallas_call(
        functools.partial(weight_kernel, bool(small)),
        in_specs=[VMEM] * (HALVES + 1 + len(small)),
        out_specs=VMEM,
        out_shape=jax.ShapeDtypeStruct((rows, d // 2), F32),
        compiler_params=params(16),
        cost_estimate=cost(m * h * d * g, m * g * (2 * h + d) + 2 * h * d),
        name="theirs" if small else "mine",
    )(*gps, state, *small)


def blocks_kernel(mine_ref, got_ref, small_ref, out_ref):
    core = lax.rem(lax.axis_index("ens"), 2)
    h, columns = mine_ref.shape
    own = pl.ds(pl.multiple_of(core * columns, columns), columns)

    def fill(order):
        for place, block in enumerate(order):
            k, j = divmod(place, 8)
            rows = slice(16 * block, 16 * block + 16)
            out_ref[k, 16 * j : 16 * j + 16, :] = mine_ref[rows, :] + got_ref[rows, :]

    pl.when(core == 0)(lambda: fill(ORDER[0]))
    pl.when(core != 0)(lambda: fill(ORDER[1]))
    for k in range(8):
        rows = slice(16 * k, 16 * k + 16)
        out_ref[k, 128:, :] = small_ref[rows, own] + got_ref[h + 16 * k : h + 16 * k + 16, :]


def make_blocks(mine, got, small):
    return pl.pallas_call(
        blocks_kernel,
        in_specs=[VMEM] * 3,
        out_specs=VMEM,
        out_shape=jax.ShapeDtypeStruct((8, 144, 512), F32),
        compiler_params=params(16),
        cost_estimate=cost(1 << 19, 7 << 20),
        name="blocks",
    )(mine, got, small)


def latent_kernel(w_ref, *refs):
    gps, out_ref = refs[:HALVES], refs[HALVES]
    n = gps[0].shape[2]
    for k, gp in enumerate(gps):
        out_ref[0, :, k * n : (k + 1) * n] = dot(w_ref[...], gp[0]).astype(BF16)


def latent(wt, gps):
    m, h, n = gps[0].shape
    d = wt.shape[0]
    return pl.pallas_call(
        latent_kernel,
        grid=(m, d // CHUNK),
        in_specs=[pl.BlockSpec((CHUNK, h), lambda i, j: (j, 0))]
        + [pl.BlockSpec((1, h, n), lambda i, j: (i, 0, 0))] * HALVES,
        out_specs=pl.BlockSpec((1, CHUNK, HALVES * n), lambda i, j: (i, j, 0)),
        out_shape=jax.ShapeDtypeStruct((m, d, HALVES * n), BF16),
        compiler_params=params(),
        cost_estimate=cost(2 * m * h * d * n * HALVES, 2 * m * n * HALVES * (h + d)),
        name="latent",
    )(wt, *gps)


def shards(encoded_state, observed_state, location_importance, w_in, b_in, final_matrix):
    members = encoded_state.shape[0] * lax.axis_size("ens")
    points = encoded_state.shape[2] * lax.axis_size("grid")
    bias = b_in.reshape(-1, 128)
    location = location_importance.reshape(1, -1)
    factor = (1.0 - (1.0 - fair_alpha) / members) / (members - 1)

    hiddens, slopes, fcs = [], [], []
    weight = w_in
    for half in range(HALVES):
        hidden, slope, fc, *kept = forward(encoded_state, weight, bias, final_matrix, half, half == 0)
        if kept:
            weight, bias = kept
        hiddens.append(hidden)
        slopes.append(slope)
        fcs.append((fc, lax.ppermute(fc, AXES, SWAP_Z), lax.ppermute(fc, AXES, SWAP_CORE)))
    gps, init = [], ()
    for half in range(HALVES):
        fc, across, beside = fcs[half]
        if gps:
            across, gps[-1] = lax.optimization_barrier((across, gps[-1]))
        else:
            across, hiddens[-1] = lax.optimization_barrier((across, hiddens[-1]))
        everyone = (fc, beside, across, lax.ppermute(across, AXES, SWAP_CORE))
        gp, small = backward(
            everyone, observed_state, location, final_matrix, slopes[half], hiddens[half], init, factor, half
        )
        init = (small,)
        gps.append(gp)
    theirs = weight_half(gps, encoded_state, small)
    got = lax.ppermute(theirs, AXES, SWAP_CORE)
    blocks = make_blocks(weight_half(gps, encoded_state), got, small)
    blocks, late_weight = lax.optimization_barrier((blocks, w_in))
    first = all_to_all(blocks, CUBES[0])
    first, latent_sensitivity = lax.optimization_barrier((first, latent(late_weight.T, gps)))

    core = lax.axis_index("ens") % 2
    x = lax.axis_index("grid") % 4
    y = (lax.axis_index("grid") // 4) % 4
    first = jnp.sum(first, 0)
    rows, small = first[:128], first[128:]
    split = jnp.broadcast_to(rows.reshape(8, 1, 16, 512), (8, 2, 16, 512)).reshape(8, 32, 512)
    whole = jnp.broadcast_to(rows.reshape(4, 1, 32, 512), (4, 2, 32, 512)).reshape(8, 32, 512)
    send = jnp.concatenate(
        [jnp.where(core == 0, split, whole), jnp.broadcast_to(small[None], (8, 16, 512))], 1
    )
    second = jnp.sum(all_to_all(send, CUBES[1]), 0)
    send = jnp.concatenate([second[32:], second[:16]], 0)
    third = all_to_all(jnp.broadcast_to(send[None], (8, 32, 512)), CUBES[0])
    digits = jnp.asarray(np.array(HIGH[0], np.int32))
    pair = lax.dynamic_slice_in_dim(third[:, 16:], 2 * (digits[x] * 2 + digits[y]), 2, 0).reshape(32, 512)
    done = jnp.concatenate([jnp.where(core == 0, pair, second[:32]), third[:, :16].reshape(128, 512)], 0)
    other = lax.ppermute(done, AXES, SWAP_CORE)
    grad_scale = 1.0 / math.sqrt(members * points)
    total = grad_scale * jnp.where(
        core == 0, jnp.concatenate([done, other], 1), jnp.concatenate([other, done], 1)
    )
    return latent_sensitivity, total[:32], total[32:112], total[112]


def solution(mesh):
    placed = (P("ens", None, "grid"), P(None, "grid"), P("grid"), P(), P(), P())
    return jax.shard_map(
        shards,
        mesh=mesh,
        in_specs=placed,
        out_specs=(P("ens", None, "grid"), P("grid", None), P(), P()),
        check_vma=False,
    )
```

```python
import functools
import math

import jax
import jax.numpy as jnp
from jax import lax
from jax.experimental import pallas as pl
from jax.experimental.pallas import tpu as pltpu
from jax.sharding import PartitionSpec as P


delta_abs = 0.1
fair_alpha = 0.95
AXES = ("ens", "grid")
F32, BF16 = jnp.float32, jnp.bfloat16
HALVES = 2
ROOT = math.sqrt(2.0 / math.pi)
CUBIC = 0.044715
CHUNK = 512
FIRST, LATER = 48, 36


def decode(index):
    e, g = divmod(index, 32)
    zl, c = divmod(e, 2)
    zh, r = divmod(g, 16)
    y, x = divmod(r, 4)
    return x, y, zh * 2 + zl, c


def encode(x, y, z, c):
    return ((z % 2) * 2 + c) * 32 + (z // 2) * 16 + y * 4 + x


SWAP_CORE = [(i, encode(*decode(i)[:3], 1 - decode(i)[3])) for i in range(128)]
SWAP_Z = [(i, encode(decode(i)[0], decode(i)[1], decode(i)[2] ^ 1, decode(i)[3])) for i in range(128)]
HIGH = ((0, 1, 1, 0), (0, 0, 1, 1))
LOW = ((0, 0, 1, 1), (0, 1, 1, 0))


def cubes(stage):
    found = {}
    for index in range(128):
        x, y, z, c = decode(index)
        digits, others = (HIGH, LOW) if stage == 0 else (LOW, HIGH)
        place = (digits[c][x], digits[c][y], digits[1 - c][z])
        rest = (others[c][x], others[c][y], others[1 - c][z])
        found.setdefault((c, rest), []).append((place, index))
    return [[index for _, index in sorted(v)] for _, v in sorted(found.items())]


CUBES = (cubes(0), cubes(1))


def block_order(c):
    coordinate = {(HIGH[c][u], LOW[c][u]): u for u in range(4)}
    order = []
    for place in range(64):
        kx1, ky1, kz1, kx2, ky2, last = ((place >> s) & 1 for s in (5, 4, 3, 2, 1, 0))
        x, y = coordinate[kx1, kx2], coordinate[ky1, ky2]
        zh, half = (last, kz1) if c == 1 else (kz1, last)
        order.append(((zh * 4 + y) * 4 + x) * 2 + half)
    return order


ORDER = (block_order(0), block_order(1))


def all_to_all(value, groups):
    return lax.all_to_all(value, AXES, 0, 0, axis_index_groups=groups, tiled=True)


def dot(a, b):
    return jnp.dot(a, b, preferred_element_type=F32)


def dot_nt(a, b):
    return lax.dot_general(a, b, (((1,), (1,)), ((), ())), preferred_element_type=F32)


def dot_tn(a, b):
    return lax.dot_general(a, b, (((0,), (0,)), ((), ())), preferred_element_type=F32)


def params(mib=60):
    return pltpu.CompilerParams(vmem_limit_bytes=mib << 20)


def cost(flops, bytes_accessed):
    return pl.CostEstimate(flops=flops, bytes_accessed=bytes_accessed, transcendentals=0)


def forward_rows(i, r, x, w_ref, column_ref, f_ref, hidden_ref, slope_ref):
    rows = pl.ds(r, CHUNK)
    v = dot(w_ref[rows, :], x) + column_ref[rows, :]
    v2 = v * v
    t = jnp.tanh(v * (ROOT * CUBIC * v2 + ROOT))
    a = 0.5 * t + 0.5
    hidden = (v * a).astype(BF16)
    hidden_ref[i, rows, :] = hidden
    slope_ref[i, rows, :] = a + (v * (1.5 * ROOT * CUBIC * v2 + 0.5 * ROOT)) * (1.0 - t * t)
    return dot(f_ref[:, rows], hidden)


def forward_kernel(half, first, x_any, w_any, b_any, f_any, hidden_ref, slope_ref, fc_ref, *refs):
    m, h, n = hidden_ref.shape
    starts = range(0, h, CHUNK)
    if first:
        w_ref, column_ref, x_ref, b_ref, f_ref, sems = refs
    else:
        w_ref, column_ref, f_ref, (x_ref, sems) = w_any, b_any, f_any, refs

    def copy(source, target, k):
        return pltpu.make_async_copy(source, target, sems.at[k])

    fetch_x = [copy(x_any.at[i, :, pl.ds(half * n, n)], x_ref.at[i], i) for i in range(m)]
    if first:
        fetch_b, fetch_f = copy(b_any, b_ref, m), copy(f_any, f_ref, m + 1)
        fetch_w = [copy(w_any.at[pl.ds(r, CHUNK)], w_ref.at[pl.ds(r, CHUNK)], m + 2 + j) for j, r in enumerate(starts)]
        for one in [fetch_b] + fetch_w[:1] + fetch_x[:1] + [fetch_f] + fetch_w[1:] + fetch_x[1:]:
            one.start()
        fetch_b.wait()
        turned = b_ref[...].T
        for i in range(turned.shape[1]):
            column_ref[128 * i : 128 * i + 128, :] = turned[:, i : i + 1]
    else:
        for one in fetch_x:
            one.start()
    for i in range(m):
        total = None
        fetch_x[i].wait()
        for j, r in enumerate(starts):
            if first and i == 0:
                fetch_w[j].wait()
                if j == 0:
                    fetch_f.wait()
            part = forward_rows(i, r, x_ref[i], w_ref, column_ref, f_ref, hidden_ref, slope_ref)
            total = part if total is None else total + part
        fc_ref[i] = total


VMEM = pl.BlockSpec(memory_space=pltpu.VMEM)
HBM = pl.BlockSpec(memory_space=pltpu.HBM)


def forward(state, w_in, bias, final_matrix, half, first):
    m, d, g = state.shape
    h, c = w_in.shape[0], final_matrix.shape[0]
    n = g // HALVES
    results = [
        jax.ShapeDtypeStruct((m, h, n), BF16),
        jax.ShapeDtypeStruct((m, h, n), F32),
        jax.ShapeDtypeStruct((m, c, n), F32),
    ]
    scratch = [pltpu.VMEM((m, d, n), BF16)]
    if first:
        results += [jax.ShapeDtypeStruct((h, d), BF16), jax.ShapeDtypeStruct((h, 1), F32)]
        scratch += [pltpu.VMEM(bias.shape, F32), pltpu.VMEM((c, h), BF16)]
    return pl.pallas_call(
        functools.partial(forward_kernel, half, first),
        in_specs=[HBM] * 4 if first else [HBM] + [VMEM] * 3,
        out_specs=[VMEM] * len(results),
        out_shape=results,
        scratch_shapes=scratch + [pltpu.SemaphoreType.DMA((m + 2 + h // CHUNK,))],
        compiler_params=params(FIRST if first else LATER),
        cost_estimate=cost(2 * m * h * n * (d + c), m * n * (2 * d + 6 * h)),
    )(state, w_in, bias, final_matrix)


def slope_of(d):
    return d * lax.rsqrt(d * d + delta_abs * delta_abs)


def backward_kernel(factor, half, own_ref, a_ref, b_ref, c_ref, obs_ref, loc_ref, f_ref, slope_ref, hidden_ref,
                    *refs):
    init, (gp_ref, small_ref, wide_ref, bias_ref) = refs[:-4], refs[-4:]
    m, channels, n = own_ref.shape
    here = slice(half * n, half * n + n)
    ones = jnp.ones((8, n), BF16)
    for i in range(m):
        own = own_ref[i]
        pairs = None
        for ref in (own_ref, a_ref, b_ref, c_ref):
            for k in range(m):
                s = slope_of(own - ref[k])
                pairs = s if pairs is None else pairs + s
        grad = (loc_ref[:, here] * (slope_of(own - obs_ref[:, here]) - factor * pairs)).astype(BF16)
        for r in range(0, f_ref.shape[1], CHUNK):
            rows = pl.ds(r, CHUNK)
            gp = (dot_tn(f_ref[:, rows], grad) * slope_ref[i, rows, :]).astype(BF16)
            gp_ref[i, rows, :] = gp
            wide = dot_nt(hidden_ref[i, rows, :], grad)
            bias = dot_nt(gp, ones)
            if i == 0:
                wide_ref[rows, :channels] = wide
                bias_ref[rows, :] = bias
            else:
                wide_ref[rows, :channels] += wide
                bias_ref[rows, :] += bias
    wide, bias = wide_ref[...].T[:channels, :], bias_ref[...].T
    if init:
        wide += init[0][:channels, :]
        bias += init[0][channels : channels + 8, :]
    small_ref[:channels, :] = wide
    small_ref[channels : channels + 8, :] = bias
    small_ref[channels + 8 :, :] = jnp.zeros_like(small_ref[channels + 8 :, :])


def backward(fcs, observed, location, final_matrix, slope, hidden, init, factor, half):
    m, h, n = hidden.shape
    operands = (*fcs, observed, location, final_matrix, slope, hidden, *init)
    return pl.pallas_call(
        functools.partial(backward_kernel, factor, half),
        in_specs=[VMEM] * len(operands),
        out_specs=[VMEM, VMEM],
        out_shape=[jax.ShapeDtypeStruct((m, h, n), BF16), jax.ShapeDtypeStruct((128, h), F32)],
        scratch_shapes=[
            pltpu.VMEM((h, 128), F32),
            pltpu.VMEM((h, 8), F32),
        ],
        compiler_params=params(16),
        cost_estimate=cost(4 * m * h * n * 256, m * n * 8 * h),
    )(*operands)


def weight_kernel(other, *refs):
    gps, (x_ref, *rest) = refs[:HALVES], refs[HALVES:]
    out_ref = rest[-1]
    m, h, n = gps[0].shape
    columns = out_ref.shape[1]
    core = lax.rem(lax.axis_index("ens"), 2)
    own = pl.ds(pl.multiple_of((1 - core if other else core) * columns, columns), columns)
    for r in range(0, h, CHUNK):
        rows = pl.ds(r, CHUNK)
        out_ref[rows, :] = sum(
            dot_nt(gp[i, rows, :], x_ref[i, own, k * n : (k + 1) * n]) for i in range(m) for k, gp in enumerate(gps)
        )
    if other:
        out_ref[h:, :] = rest[0][:, own]


def weight_half(gps, state, *small):
    m, d, g = state.shape
    h = gps[0].shape[1]
    rows = h + sum(one.shape[0] for one in small)
    return pl.pallas_call(
        functools.partial(weight_kernel, bool(small)),
        in_specs=[VMEM] * (HALVES + 1 + len(small)),
        out_specs=VMEM,
        out_shape=jax.ShapeDtypeStruct((rows, d // 2), F32),
        compiler_params=params(16),
        cost_estimate=cost(m * h * d * g, m * g * (2 * h + d) + 2 * h * d),
        name="theirs" if small else "mine",
    )(*gps, state, *small)


def blocks_kernel(mine_ref, got_ref, small_ref, out_ref):
    core = lax.rem(lax.axis_index("ens"), 2)
    h, columns = mine_ref.shape
    own = pl.ds(pl.multiple_of(core * columns, columns), columns)

    def fill(order):
        for place, block in enumerate(order):
            k, j = divmod(place, 8)
            rows = slice(16 * block, 16 * block + 16)
            out_ref[k, 16 * j : 16 * j + 16, :] = mine_ref[rows, :] + got_ref[rows, :]

    pl.when(core == 0)(lambda: fill(ORDER[0]))
    pl.when(core != 0)(lambda: fill(ORDER[1]))
    for k in range(8):
        rows = slice(16 * k, 16 * k + 16)
        out_ref[k, 128:, :] = small_ref[rows, own] + got_ref[h + 16 * k : h + 16 * k + 16, :]


def make_blocks(mine, got, small):
    return pl.pallas_call(
        blocks_kernel,
        in_specs=[VMEM] * 3,
        out_specs=VMEM,
        out_shape=jax.ShapeDtypeStruct((8, 144, 512), F32),
        compiler_params=params(16),
        cost_estimate=cost(1 << 19, 7 << 20),
        name="blocks",
    )(mine, got, small)


def gather_kernel(second_ref, out_ref, kept_ref):
    total = second_ref[0]
    for k in range(1, second_ref.shape[0]):
        total = total + second_ref[k]
    kept_ref[...] = total[:32]
    for k in range(out_ref.shape[0]):
        out_ref[k, :16, :] = total[32:]
        out_ref[k, 16:, :] = total[:16]


def gather_blocks(second):
    return pl.pallas_call(
        gather_kernel,
        in_specs=[VMEM],
        out_specs=[VMEM] * 2,
        out_shape=[jax.ShapeDtypeStruct((8, 32, 512), F32), jax.ShapeDtypeStruct((32, 512), F32)],
        compiler_params=params(16),
        name="gather",
    )(second)


def pick_kernel(kept_ref, third_ref, out_ref):
    core = lax.rem(lax.axis_index("ens"), 2)
    x = lax.rem(lax.axis_index("grid"), 4)
    y = lax.rem(lax.div(lax.axis_index("grid"), 4), 4)
    place = 2 * (2 * lax.div(x, 2) + lax.div(y, 2))

    @pl.when(core == 0)
    def _():
        out_ref[:32, :] = kept_ref[...]

    @pl.when(core != 0)
    def _():
        out_ref[:16, :] = third_ref[place, 16:, :]
        out_ref[16:32, :] = third_ref[place + 1, 16:, :]

    for k in range(third_ref.shape[0]):
        out_ref[32 + 16 * k : 48 + 16 * k, :] = third_ref[k, :16, :]


def pick(kept, third):
    return pl.pallas_call(
        pick_kernel,
        in_specs=[VMEM] * 2,
        out_specs=VMEM,
        out_shape=jax.ShapeDtypeStruct((160, 512), F32),
        compiler_params=params(16),
        name="pick",
    )(kept, third)


def finish_kernel(scale, done_ref, other_ref, in_ref, out_ref, bias_ref):
    core = lax.rem(lax.axis_index("ens"), 2)
    columns = done_ref.shape[1]
    for which, ref in ((core, done_ref), (1 - core, other_ref)):
        lanes = pl.ds(pl.multiple_of(columns * which, columns), columns)
        in_ref[:, lanes] = ref[:32, :] * scale
        out_ref[:, lanes] = ref[32:112, :] * scale
        bias_ref[:, lanes] = ref[112:113, :] * scale


def finish(scale, *operands):
    return pl.pallas_call(
        functools.partial(finish_kernel, scale),
        in_specs=[VMEM] * len(operands),
        out_specs=[VMEM] * 3,
        out_shape=[jax.ShapeDtypeStruct(shape, F32) for shape in ((32, 1024), (80, 1024), (1, 1024))],
        compiler_params=params(16),
        name="finish",
    )(*operands)


def latent_kernel(w_ref, *refs):
    gps, out_ref = refs[:HALVES], refs[HALVES]
    n = gps[0].shape[2]
    for k, gp in enumerate(gps):
        out_ref[0, :, k * n : (k + 1) * n] = dot(w_ref[...], gp[0]).astype(BF16)


def latent(wt, gps):
    m, h, n = gps[0].shape
    d = wt.shape[0]
    return pl.pallas_call(
        latent_kernel,
        grid=(m, d // CHUNK),
        in_specs=[pl.BlockSpec((CHUNK, h), lambda i, j: (j, 0))]
        + [pl.BlockSpec((1, h, n), lambda i, j: (i, 0, 0))] * HALVES,
        out_specs=pl.BlockSpec((1, CHUNK, HALVES * n), lambda i, j: (i, j, 0)),
        out_shape=jax.ShapeDtypeStruct((m, d, HALVES * n), BF16),
        compiler_params=params(),
        cost_estimate=cost(2 * m * h * d * n * HALVES, 2 * m * n * HALVES * (h + d)),
        name="latent",
    )(wt, *gps)


def shards(encoded_state, observed_state, location_importance, w_in, b_in, final_matrix):
    members = encoded_state.shape[0] * lax.axis_size("ens")
    points = encoded_state.shape[2] * lax.axis_size("grid")
    bias = b_in.reshape(-1, 128)
    location = location_importance.reshape(1, -1)
    factor = (1.0 - (1.0 - fair_alpha) / members) / (members - 1)

    hiddens, slopes, fcs = [], [], []
    weight = w_in
    for half in range(HALVES):
        hidden, slope, fc, *kept = forward(encoded_state, weight, bias, final_matrix, half, half == 0)
        if kept:
            weight, bias = kept
        hiddens.append(hidden)
        slopes.append(slope)
        across = lax.ppermute(fc, AXES, SWAP_Z)
        fcs.append((fc, across, lax.ppermute(fc, AXES, SWAP_CORE)))
    gps, init = [], ()
    for half in range(HALVES):
        fc, across, beside = fcs[half]
        if gps:
            across, gps[-1] = lax.optimization_barrier((across, gps[-1]))
        else:
            across, hiddens[-1] = lax.optimization_barrier((across, hiddens[-1]))
        diagonal = lax.ppermute(across, AXES, SWAP_CORE)
        everyone = (fc, beside, across, diagonal)
        gp, small = backward(
            everyone, observed_state, location, final_matrix, slopes[half], hiddens[half], init, factor, half
        )
        init = (small,)
        gps.append(gp)
    theirs = weight_half(gps, encoded_state, small)
    got = lax.ppermute(theirs, AXES, SWAP_CORE)
    blocks = make_blocks(weight_half(gps, encoded_state), got, small)
    blocks, late_weight = lax.optimization_barrier((blocks, w_in))
    first = all_to_all(blocks, CUBES[0])
    first, latent_sensitivity = lax.optimization_barrier((first, latent(late_weight.T, gps)))

    core = lax.axis_index("ens") % 2
    first = jnp.sum(first, 0)
    rows, small = first[:128], first[128:]
    split = jnp.broadcast_to(rows.reshape(8, 1, 16, 512), (8, 2, 16, 512)).reshape(8, 32, 512)
    whole = jnp.broadcast_to(rows.reshape(4, 1, 32, 512), (4, 2, 32, 512)).reshape(8, 32, 512)
    send = jnp.concatenate(
        [jnp.where(core == 1, split, whole), jnp.broadcast_to(small[None], (8, 16, 512))], 1
    )
    send, kept = gather_blocks(all_to_all(send, CUBES[1]))
    done = pick(kept, all_to_all(send, CUBES[0]))
    other = lax.ppermute(done, AXES, SWAP_CORE)
    in_sum, out_sum, bias_sum = finish(1.0 / math.sqrt(members * points), done, other)
    return latent_sensitivity, in_sum, out_sum, bias_sum.reshape(-1)


def solution(mesh):
    placed = (P("ens", None, "grid"), P(None, "grid"), P("grid"), P(), P(), P())
    return jax.shard_map(
        shards,
        mesh=mesh,
        in_specs=placed,
        out_specs=(P("ens", None, "grid"), P("grid", None), P(), P()),
        check_vma=False,
    )
```

```python
import functools
import math

import jax
import jax.numpy as jnp
from jax import lax
from jax.experimental import pallas as pl
from jax.experimental.pallas import tpu as pltpu
from jax.sharding import PartitionSpec as P


delta_abs = 0.1
fair_alpha = 0.95
AXES = ("ens", "grid")
F32, BF16 = jnp.float32, jnp.bfloat16
HALVES = 2
ROOT = math.sqrt(2.0 / math.pi)
CUBIC = 0.044715
CHUNK = 512
FIRST, LATER = 48, 36


def decode(index):
    e, g = divmod(index, 32)
    zl, c = divmod(e, 2)
    zh, r = divmod(g, 16)
    y, x = divmod(r, 4)
    return x, y, zh * 2 + zl, c


def encode(x, y, z, c):
    return ((z % 2) * 2 + c) * 32 + (z // 2) * 16 + y * 4 + x


SWAP_CORE = [(i, encode(*decode(i)[:3], 1 - decode(i)[3])) for i in range(128)]
SWAP_Z = [(i, encode(decode(i)[0], decode(i)[1], decode(i)[2] ^ 1, decode(i)[3])) for i in range(128)]
HIGH = ((0, 1, 1, 0), (0, 0, 1, 1))
LOW = ((0, 0, 1, 1), (0, 1, 1, 0))


def cubes(stage):
    found = {}
    for index in range(128):
        x, y, z, c = decode(index)
        digits, others = (HIGH, LOW) if stage == 0 else (LOW, HIGH)
        place = (digits[c][x], digits[c][y], digits[1 - c][z])
        rest = (others[c][x], others[c][y], others[1 - c][z])
        found.setdefault((c, rest), []).append((place, index))
    return [[index for _, index in sorted(v)] for _, v in sorted(found.items())]


CUBES = (cubes(0), cubes(1))


def block_order(c):
    coordinate = {(HIGH[c][u], LOW[c][u]): u for u in range(4)}
    order = []
    for place in range(64):
        kx1, ky1, kz1, kx2, ky2, last = ((place >> s) & 1 for s in (5, 4, 3, 2, 1, 0))
        x, y = coordinate[kx1, kx2], coordinate[ky1, ky2]
        zh, half = (last, kz1) if c == 1 else (kz1, last)
        order.append(((zh * 4 + y) * 4 + x) * 2 + half)
    return order


ORDER = (block_order(0), block_order(1))


def all_to_all(value, groups):
    return lax.all_to_all(value, AXES, 0, 0, axis_index_groups=groups, tiled=True)


def dot(a, b):
    return jnp.dot(a, b, preferred_element_type=F32)


def dot_nt(a, b):
    return lax.dot_general(a, b, (((1,), (1,)), ((), ())), preferred_element_type=F32)


def dot_tn(a, b):
    return lax.dot_general(a, b, (((0,), (0,)), ((), ())), preferred_element_type=F32)


def params(mib=60):
    return pltpu.CompilerParams(vmem_limit_bytes=int(mib * 1048576))


def cost(flops, bytes_accessed):
    return pl.CostEstimate(flops=flops, bytes_accessed=bytes_accessed, transcendentals=0)


def forward_rows(i, r, x, w_ref, column_ref, f_ref, hidden_ref, slope_ref):
    rows = pl.ds(r, CHUNK)
    v = dot(w_ref[rows, :], x) + column_ref[rows, :]
    v2 = v * v
    t = jnp.tanh(v * (ROOT * CUBIC * v2 + ROOT))
    a = 0.5 * t + 0.5
    hidden = (v * a).astype(BF16)
    hidden_ref[i, rows, :] = hidden
    slope_ref[i, rows, :] = a + (v * (1.5 * ROOT * CUBIC * v2 + 0.5 * ROOT)) * (1.0 - t * t)
    return dot(f_ref[:, rows], hidden)


def forward_kernel(half, first, x_any, w_any, b_any, f_any, hidden_ref, slope_ref, fc_ref, *refs):
    m, h, n = hidden_ref.shape
    starts = range(0, h, CHUNK)
    if first:
        w_ref, column_ref, x_ref, b_ref, f_ref, sems = refs
    else:
        w_ref, column_ref, f_ref, (x_ref, sems) = w_any, b_any, f_any, refs

    def copy(source, target, k):
        return pltpu.make_async_copy(source, target, sems.at[k])

    fetch_x = [copy(x_any.at[i, :, pl.ds(half * n, n)], x_ref.at[i], i) for i in range(m)]
    if first:
        fetch_b, fetch_f = copy(b_any, b_ref, m), copy(f_any, f_ref, m + 1)
        fetch_w = [copy(w_any.at[pl.ds(r, CHUNK)], w_ref.at[pl.ds(r, CHUNK)], m + 2 + j) for j, r in enumerate(starts)]
        for one in [fetch_b] + fetch_w[:1] + fetch_x[:1] + [fetch_f] + fetch_w[1:] + fetch_x[1:]:
            one.start()
        fetch_b.wait()
        turned = b_ref[...].T
        for i in range(turned.shape[1]):
            column_ref[128 * i : 128 * i + 128, :] = turned[:, i : i + 1]
    else:
        for one in fetch_x:
            one.start()
    for i in range(m):
        total = None
        fetch_x[i].wait()
        for j, r in enumerate(starts):
            if first and i == 0:
                fetch_w[j].wait()
                if j == 0:
                    fetch_f.wait()
            part = forward_rows(i, r, x_ref[i], w_ref, column_ref, f_ref, hidden_ref, slope_ref)
            total = part if total is None else total + part
        fc_ref[i] = total


VMEM = pl.BlockSpec(memory_space=pltpu.VMEM)
HBM = pl.BlockSpec(memory_space=pltpu.HBM)


def forward(state, w_in, bias, final_matrix, half, first):
    m, d, g = state.shape
    h, c = w_in.shape[0], final_matrix.shape[0]
    n = g // HALVES
    results = [
        jax.ShapeDtypeStruct((m, h, n), BF16),
        jax.ShapeDtypeStruct((m, h, n), F32),
        jax.ShapeDtypeStruct((m, c, n), F32),
    ]
    scratch = [pltpu.VMEM((m, d, n), BF16)]
    if first:
        results += [jax.ShapeDtypeStruct((h, d), BF16), jax.ShapeDtypeStruct((h, 1), F32)]
        scratch += [pltpu.VMEM(bias.shape, F32), pltpu.VMEM((c, h), BF16)]
    return pl.pallas_call(
        functools.partial(forward_kernel, half, first),
        in_specs=[HBM] * 4 if first else [HBM] + [VMEM] * 3,
        out_specs=[VMEM] * len(results),
        out_shape=results,
        scratch_shapes=scratch + [pltpu.SemaphoreType.DMA((m + 2 + h // CHUNK,))],
        compiler_params=params(FIRST if first else LATER),
        cost_estimate=cost(2 * m * h * n * (d + c), m * n * (2 * d + 6 * h)),
    )(state, w_in, bias, final_matrix)


def slope_of(d):
    return d * lax.rsqrt(d * d + delta_abs * delta_abs)


def backward_kernel(factor, half, own_ref, a_ref, b_ref, c_ref, obs_ref, loc_ref, f_ref, slope_ref, hidden_ref,
                    *refs):
    init, (gp_ref, small_ref, wide_ref, bias_ref) = refs[:-4], refs[-4:]
    m, channels, n = own_ref.shape
    here = slice(half * n, half * n + n)
    ones = jnp.ones((8, n), BF16)
    for i in range(m):
        own = own_ref[i]
        pairs = None
        for ref in (own_ref, a_ref, b_ref, c_ref):
            for k in range(m):
                s = slope_of(own - ref[k])
                pairs = s if pairs is None else pairs + s
        grad = (loc_ref[:, here] * (slope_of(own - obs_ref[:, here]) - factor * pairs)).astype(BF16)
        for r in range(0, f_ref.shape[1], CHUNK):
            rows = pl.ds(r, CHUNK)
            gp = (dot_tn(f_ref[:, rows], grad) * slope_ref[i, rows, :]).astype(BF16)
            gp_ref[i, rows, :] = gp
            wide = dot_nt(hidden_ref[i, rows, :], grad)
            bias = dot_nt(gp, ones)
            if i == 0:
                wide_ref[rows, :channels] = wide
                bias_ref[rows, :] = bias
            else:
                wide_ref[rows, :channels] += wide
                bias_ref[rows, :] += bias
    wide, bias = wide_ref[...].T[:channels, :], bias_ref[...].T
    if init:
        wide += init[0][:channels, :]
        bias += init[0][channels : channels + 8, :]
    small_ref[:channels, :] = wide
    small_ref[channels : channels + 8, :] = bias
    small_ref[channels + 8 :, :] = jnp.zeros_like(small_ref[channels + 8 :, :])


def backward(fcs, observed, location, final_matrix, slope, hidden, init, factor, half):
    m, h, n = hidden.shape
    operands = (*fcs, observed, location, final_matrix, slope, hidden, *init)
    return pl.pallas_call(
        functools.partial(backward_kernel, factor, half),
        in_specs=[VMEM] * len(operands),
        out_specs=[VMEM, VMEM],
        out_shape=[jax.ShapeDtypeStruct((m, h, n), BF16), jax.ShapeDtypeStruct((128, h), F32)],
        scratch_shapes=[
            pltpu.VMEM((h, 128), F32),
            pltpu.VMEM((h, 8), F32),
        ],
        compiler_params=params(16),
        cost_estimate=cost(4 * m * h * n * 256, m * n * 8 * h),
    )(*operands)


def weight_kernel(other, begin, end, *refs):
    gps, (x_ref, *rest) = refs[:HALVES], refs[HALVES:]
    out_ref = rest[-1]
    m, _, n = gps[0].shape
    columns = out_ref.shape[1]
    core = lax.rem(lax.axis_index("ens"), 2)
    own = pl.ds(pl.multiple_of((1 - core if other else core) * columns, columns), columns)
    for r in range(begin, end, CHUNK):
        rows = pl.ds(r, CHUNK)
        out_ref[r - begin : r - begin + CHUNK, :] = sum(
            dot_nt(gp[i, rows, :], x_ref[i, own, k * n : (k + 1) * n]) for i in range(m) for k, gp in enumerate(gps)
        )
    if len(rest) > 1:
        out_ref[end - begin :, :] = rest[0][:, own]


def weight_half(gps, state, other, begin, end, *small):
    m, d, g = state.shape
    rows = end - begin + sum(one.shape[0] for one in small)
    return pl.pallas_call(
        functools.partial(weight_kernel, other, begin, end),
        in_specs=[VMEM] * (HALVES + 1 + len(small)),
        out_specs=VMEM,
        out_shape=jax.ShapeDtypeStruct((rows, d // 2), F32),
        compiler_params=params(16),
        cost_estimate=cost(m * (end - begin) * d * g, m * g * (2 * (end - begin) + d) + 2 * rows * d),
    )(*gps, state, *small)


def blocks_kernel(mine_ref, low_ref, high_ref, small_ref, out_ref):
    core = lax.rem(lax.axis_index("ens"), 2)
    h, columns = mine_ref.shape
    own = pl.ds(pl.multiple_of(core * columns, columns), columns)

    def fill(order):
        for place, block in enumerate(order):
            k, j = divmod(place, 8)
            rows = slice(16 * block, 16 * block + 16)
            got_ref, start = (low_ref, 0) if 16 * block < h // 2 else (high_ref, h // 2)
            got = got_ref[16 * block - start : 16 * block - start + 16, :]
            out_ref[k, 16 * j : 16 * j + 16, :] = mine_ref[rows, :] + got

    pl.when(core == 0)(lambda: fill(ORDER[0]))
    pl.when(core != 0)(lambda: fill(ORDER[1]))
    for k in range(8):
        rows = slice(16 * k, 16 * k + 16)
        out_ref[k, 128:, :] = small_ref[rows, own] + high_ref[h // 2 + 16 * k : h // 2 + 16 * k + 16, :]


def make_blocks(mine, low, high, small):
    return pl.pallas_call(
        blocks_kernel,
        in_specs=[VMEM] * 4,
        out_specs=VMEM,
        out_shape=jax.ShapeDtypeStruct((8, 144, 512), F32),
        compiler_params=params(16),
        cost_estimate=cost(1 << 19, 7 << 20),
        name="blocks",
    )(mine, low, high, small)


def gather_kernel(second_ref, out_ref, kept_ref):
    total = second_ref[0]
    for k in range(1, second_ref.shape[0]):
        total = total + second_ref[k]
    kept_ref[...] = total[:32]
    for k in range(out_ref.shape[0]):
        out_ref[k, :16, :] = total[32:]
        out_ref[k, 16:, :] = total[:16]


def gather_blocks(second):
    return pl.pallas_call(
        gather_kernel,
        in_specs=[VMEM],
        out_specs=[VMEM] * 2,
        out_shape=[jax.ShapeDtypeStruct((8, 32, 512), F32), jax.ShapeDtypeStruct((32, 512), F32)],
        compiler_params=params(16),
        name="gather",
    )(second)


def pick_kernel(kept_ref, third_ref, out_ref):
    core = lax.rem(lax.axis_index("ens"), 2)
    x = lax.rem(lax.axis_index("grid"), 4)
    y = lax.rem(lax.div(lax.axis_index("grid"), 4), 4)
    place = 2 * (2 * lax.div(x, 2) + lax.div(y, 2))

    @pl.when(core == 0)
    def _():
        out_ref[:32, :] = kept_ref[...]

    @pl.when(core != 0)
    def _():
        out_ref[:16, :] = third_ref[place, 16:, :]
        out_ref[16:32, :] = third_ref[place + 1, 16:, :]

    for k in range(third_ref.shape[0]):
        out_ref[32 + 16 * k : 48 + 16 * k, :] = third_ref[k, :16, :]


def pick(kept, third):
    return pl.pallas_call(
        pick_kernel,
        in_specs=[VMEM] * 2,
        out_specs=VMEM,
        out_shape=jax.ShapeDtypeStruct((160, 512), F32),
        compiler_params=params(16),
        name="pick",
    )(kept, third)


def finish_kernel(scale, done_ref, other_ref, in_ref, out_ref, bias_ref):
    core = lax.rem(lax.axis_index("ens"), 2)
    columns = done_ref.shape[1]
    for which, ref in ((core, done_ref), (1 - core, other_ref)):
        lanes = pl.ds(pl.multiple_of(columns * which, columns), columns)
        in_ref[:, lanes] = ref[:32, :] * scale
        out_ref[:, lanes] = ref[32:112, :] * scale
        bias_ref[:, lanes] = ref[112:113, :] * scale


def finish(scale, *operands):
    return pl.pallas_call(
        functools.partial(finish_kernel, scale),
        in_specs=[VMEM] * len(operands),
        out_specs=[VMEM] * 3,
        out_shape=[jax.ShapeDtypeStruct(shape, F32) for shape in ((32, 1024), (80, 1024), (1, 1024))],
        compiler_params=params(16),
        name="finish",
    )(*operands)


def latent_kernel(w_ref, *refs):
    gps, out_ref = refs[:HALVES], refs[HALVES]
    n = gps[0].shape[2]
    for k, gp in enumerate(gps):
        out_ref[0, :, k * n : (k + 1) * n] = dot(w_ref[...], gp[0]).astype(BF16)


def latent(wt, gps):
    m, h, n = gps[0].shape
    d = wt.shape[0]
    return pl.pallas_call(
        latent_kernel,
        grid=(m, d // CHUNK),
        in_specs=[pl.BlockSpec((CHUNK, h), lambda i, j: (j, 0))]
        + [pl.BlockSpec((1, h, n), lambda i, j: (i, 0, 0))] * HALVES,
        out_specs=pl.BlockSpec((1, CHUNK, HALVES * n), lambda i, j: (i, j, 0)),
        out_shape=jax.ShapeDtypeStruct((m, d, HALVES * n), BF16),
        compiler_params=params(),
        cost_estimate=cost(2 * m * h * d * n * HALVES, 2 * m * n * HALVES * (h + d)),
        name="latent",
    )(wt, *gps)


def shards(encoded_state, observed_state, location_importance, w_in, b_in, final_matrix):
    members = encoded_state.shape[0] * lax.axis_size("ens")
    points = encoded_state.shape[2] * lax.axis_size("grid")
    bias = b_in.reshape(-1, 128)
    location = location_importance.reshape(1, -1)
    factor = (1.0 - (1.0 - fair_alpha) / members) / (members - 1)

    hiddens, slopes, fcs = [], [], []
    weight = w_in
    for half in range(HALVES):
        hidden, slope, fc, *kept = forward(encoded_state, weight, bias, final_matrix, half, half == 0)
        if kept:
            weight, bias = kept
        hiddens.append(hidden)
        slopes.append(slope)
        across = lax.ppermute(fc, AXES, SWAP_Z)
        fcs.append((fc, across, lax.ppermute(fc, AXES, SWAP_CORE)))
    gps, init = [], ()
    for half in range(HALVES):
        fc, across, beside = fcs[half]
        if gps:
            across, gps[-1] = lax.optimization_barrier((across, gps[-1]))
        else:
            across, hiddens[-1] = lax.optimization_barrier((across, hiddens[-1]))
        diagonal = lax.ppermute(across, AXES, SWAP_CORE)
        everyone = (fc, beside, across, diagonal)
        gp, small = backward(
            everyone, observed_state, location, final_matrix, slopes[half], hiddens[half], init, factor, half
        )
        init = (small,)
        gps.append(gp)
    units = w_in.shape[0]
    low = weight_half(gps, encoded_state, True, 0, units // 2)
    low = lax.ppermute(low, AXES, SWAP_CORE)
    high = weight_half(gps, encoded_state, True, units // 2, units, small)
    high = lax.ppermute(high, AXES, SWAP_CORE)
    own = weight_half(gps, encoded_state, False, 0, units)
    blocks = make_blocks(own, low, high, small)
    blocks, late_weight = lax.optimization_barrier((blocks, w_in))
    first = all_to_all(blocks, CUBES[0])
    first, latent_sensitivity = lax.optimization_barrier((first, latent(late_weight.T, gps)))

    core = lax.axis_index("ens") % 2
    first = jnp.sum(first, 0)
    rows, small = first[:128], first[128:]
    split = jnp.broadcast_to(rows.reshape(8, 1, 16, 512), (8, 2, 16, 512)).reshape(8, 32, 512)
    whole = jnp.broadcast_to(rows.reshape(4, 1, 32, 512), (4, 2, 32, 512)).reshape(8, 32, 512)
    send = jnp.concatenate(
        [jnp.where(core == 1, split, whole), jnp.broadcast_to(small[None], (8, 16, 512))], 1
    )
    send, kept = gather_blocks(all_to_all(send, CUBES[1]))
    done = pick(kept, all_to_all(send, CUBES[0]))
    other = lax.ppermute(done, AXES, SWAP_CORE)
    in_sum, out_sum, bias_sum = finish(1.0 / math.sqrt(members * points), done, other)
    return latent_sensitivity, in_sum, out_sum, bias_sum.reshape(-1)


def solution(mesh):
    placed = (P("ens", None, "grid"), P(None, "grid"), P("grid"), P(), P(), P())
    return jax.shard_map(
        shards,
        mesh=mesh,
        in_specs=placed,
        out_specs=(P("ens", None, "grid"), P("grid", None), P(), P()),
        check_vma=False,
    )
```

```python
import functools
import math

import jax
import jax.numpy as jnp
from jax import lax
from jax.experimental import pallas as pl
from jax.experimental.pallas import tpu as pltpu
from jax.sharding import PartitionSpec as P


delta_abs = 0.1
fair_alpha = 0.95
AXES = ("ens", "grid")
F32, BF16 = jnp.float32, jnp.bfloat16
HALVES = 2
ROOT = math.sqrt(2.0 / math.pi)
CUBIC = 0.044715
CHUNK = 512
ROWS = 1024
FIRST, LATER = 48, 36


def decode(index):
    e, g = divmod(index, 32)
    zl, c = divmod(e, 2)
    zh, r = divmod(g, 16)
    y, x = divmod(r, 4)
    return x, y, zh * 2 + zl, c


def encode(x, y, z, c):
    return ((z % 2) * 2 + c) * 32 + (z // 2) * 16 + y * 4 + x


SWAP_CORE = [(i, encode(*decode(i)[:3], 1 - decode(i)[3])) for i in range(128)]
SWAP_Z = [(i, encode(decode(i)[0], decode(i)[1], decode(i)[2] ^ 1, decode(i)[3])) for i in range(128)]
HIGH = ((0, 1, 1, 0), (0, 0, 1, 1))
LOW = ((0, 0, 1, 1), (0, 1, 1, 0))


def cubes(stage):
    found = {}
    for index in range(128):
        x, y, z, c = decode(index)
        digits, others = (HIGH, LOW) if stage == 0 else (LOW, HIGH)
        place = (digits[c][x], digits[c][y], digits[1 - c][z])
        rest = (others[c][x], others[c][y], others[1 - c][z])
        found.setdefault((c, rest), []).append((place, index))
    return [[index for _, index in sorted(v)] for _, v in sorted(found.items())]


CUBES = (cubes(0), cubes(1))


def block_order(c):
    coordinate = {(HIGH[c][u], LOW[c][u]): u for u in range(4)}
    order = []
    for place in range(64):
        kx1, ky1, kz1, kx2, ky2, last = ((place >> s) & 1 for s in (5, 4, 3, 2, 1, 0))
        x, y = coordinate[kx1, kx2], coordinate[ky1, ky2]
        zh, half = (last, kz1) if c == 1 else (kz1, last)
        order.append(((zh * 4 + y) * 4 + x) * 2 + half)
    return order


ORDER = (block_order(0), block_order(1))


def all_to_all(value, groups):
    return lax.all_to_all(value, AXES, 0, 0, axis_index_groups=groups, tiled=True)


def dot(a, b):
    return jnp.dot(a, b, preferred_element_type=F32)


def dot_nt(a, b):
    return lax.dot_general(a, b, (((1,), (1,)), ((), ())), preferred_element_type=F32)


def dot_tn(a, b):
    return lax.dot_general(a, b, (((0,), (0,)), ((), ())), preferred_element_type=F32)


def params(mib=60):
    return pltpu.CompilerParams(vmem_limit_bytes=int(mib * 1048576))


def cost(flops, bytes_accessed):
    return pl.CostEstimate(flops=flops, bytes_accessed=bytes_accessed, transcendentals=0)


def forward_rows(i, r, x, w_ref, column_ref, f_ref, hidden_ref, slope_ref):
    rows = pl.ds(r, ROWS)
    v = dot(w_ref[rows, :], x) + column_ref[rows, :]
    v2 = v * v
    t = jnp.tanh(v * (ROOT * CUBIC * v2 + ROOT))
    a = 0.5 * t + 0.5
    hidden = (v * a).astype(BF16)
    hidden_ref[i, rows, :] = hidden
    slope_ref[i, rows, :] = a + (v * (1.5 * ROOT * CUBIC * v2 + 0.5 * ROOT)) * (1.0 - t * t)
    return dot(f_ref[:, rows], hidden)


def forward_kernel(half, first, x_any, w_any, b_any, f_any, hidden_ref, slope_ref, fc_ref, *refs):
    m, h, n = hidden_ref.shape
    starts = range(0, h, ROWS)
    if first:
        w_ref, column_ref, x_ref, b_ref, f_ref, sems = refs
    else:
        w_ref, column_ref, f_ref, (x_ref, sems) = w_any, b_any, f_any, refs

    def copy(source, target, k):
        return pltpu.make_async_copy(source, target, sems.at[k])

    fetch_x = [copy(x_any.at[i, :, pl.ds(half * n, n)], x_ref.at[i], i) for i in range(m)]
    if first:
        fetch_b, fetch_f = copy(b_any, b_ref, m), copy(f_any, f_ref, m + 1)
        fetch_w = [copy(w_any.at[pl.ds(r, ROWS)], w_ref.at[pl.ds(r, ROWS)], m + 2 + j) for j, r in enumerate(starts)]
        for one in [fetch_b] + fetch_w[:1] + fetch_x[:1] + [fetch_f] + fetch_w[1:] + fetch_x[1:]:
            one.start()
        fetch_b.wait()
        turned = b_ref[...].T
        for i in range(turned.shape[1]):
            column_ref[128 * i : 128 * i + 128, :] = turned[:, i : i + 1]
    else:
        for one in fetch_x:
            one.start()
    for i in range(m):
        total = None
        fetch_x[i].wait()
        for j, r in enumerate(starts):
            if first and i == 0:
                fetch_w[j].wait()
                if j == 0:
                    fetch_f.wait()
            part = forward_rows(i, r, x_ref[i], w_ref, column_ref, f_ref, hidden_ref, slope_ref)
            total = part if total is None else total + part
        fc_ref[i] = total


VMEM = pl.BlockSpec(memory_space=pltpu.VMEM)
HBM = pl.BlockSpec(memory_space=pltpu.HBM)


def forward(state, w_in, bias, final_matrix, half, first):
    m, d, g = state.shape
    h, c = w_in.shape[0], final_matrix.shape[0]
    n = g // HALVES
    results = [
        jax.ShapeDtypeStruct((m, h, n), BF16),
        jax.ShapeDtypeStruct((m, h, n), F32),
        jax.ShapeDtypeStruct((m, c, n), F32),
    ]
    scratch = [pltpu.VMEM((m, d, n), BF16)]
    if first:
        results += [jax.ShapeDtypeStruct((h, d), BF16), jax.ShapeDtypeStruct((h, 1), F32)]
        scratch += [pltpu.VMEM(bias.shape, F32), pltpu.VMEM((c, h), BF16)]
    return pl.pallas_call(
        functools.partial(forward_kernel, half, first),
        in_specs=[HBM] * 4 if first else [HBM] + [VMEM] * 3,
        out_specs=[VMEM] * len(results),
        out_shape=results,
        scratch_shapes=scratch + [pltpu.SemaphoreType.DMA((m + 2 + h // ROWS,))],
        compiler_params=params(FIRST if first else LATER),
        cost_estimate=cost(2 * m * h * n * (d + c), m * n * (2 * d + 6 * h)),
    )(state, w_in, bias, final_matrix)


def slope_of(d):
    return d * lax.rsqrt(d * d + delta_abs * delta_abs)


def backward_kernel(factor, half, own_ref, a_ref, b_ref, c_ref, obs_ref, loc_ref, f_ref, slope_ref, hidden_ref,
                    *refs):
    init, (gp_ref, small_ref, wide_ref, bias_ref) = refs[:-4], refs[-4:]
    m, channels, n = own_ref.shape
    here = slice(half * n, half * n + n)
    ones = jnp.ones((8, n), BF16)
    for i in range(m):
        own = own_ref[i]
        pairs = None
        for ref in (own_ref, a_ref, b_ref, c_ref):
            for k in range(m):
                s = slope_of(own - ref[k])
                pairs = s if pairs is None else pairs + s
        grad = (loc_ref[:, here] * (slope_of(own - obs_ref[:, here]) - factor * pairs)).astype(BF16)
        for r in range(0, f_ref.shape[1], CHUNK):
            rows = pl.ds(r, CHUNK)
            gp = (dot_tn(f_ref[:, rows], grad) * slope_ref[i, rows, :]).astype(BF16)
            gp_ref[i, rows, :] = gp
            wide = dot_nt(hidden_ref[i, rows, :], grad)
            bias = dot_nt(gp, ones)
            if i == 0:
                wide_ref[rows, :channels] = wide
                bias_ref[rows, :] = bias
            else:
                wide_ref[rows, :channels] += wide
                bias_ref[rows, :] += bias
    wide, bias = wide_ref[...].T[:channels, :], bias_ref[...].T
    if init:
        wide += init[0][:channels, :]
        bias += init[0][channels : channels + 8, :]
    small_ref[:channels, :] = wide
    small_ref[channels : channels + 8, :] = bias
    small_ref[channels + 8 :, :] = jnp.zeros_like(small_ref[channels + 8 :, :])


def backward(fcs, observed, location, final_matrix, slope, hidden, init, factor, half):
    m, h, n = hidden.shape
    operands = (*fcs, observed, location, final_matrix, slope, hidden, *init)
    return pl.pallas_call(
        functools.partial(backward_kernel, factor, half),
        in_specs=[VMEM] * len(operands),
        out_specs=[VMEM, VMEM],
        out_shape=[jax.ShapeDtypeStruct((m, h, n), BF16), jax.ShapeDtypeStruct((128, h), F32)],
        scratch_shapes=[
            pltpu.VMEM((h, 128), F32),
            pltpu.VMEM((h, 8), F32),
        ],
        compiler_params=params(16),
        cost_estimate=cost(4 * m * h * n * 256, m * n * 8 * h),
    )(*operands)


def weight_kernel(other, begin, end, *refs):
    gps, (x_ref, *rest) = refs[:HALVES], refs[HALVES:]
    out_ref = rest[-1]
    m, _, n = gps[0].shape
    columns = out_ref.shape[1]
    core = lax.rem(lax.axis_index("ens"), 2)
    own = pl.ds(pl.multiple_of((1 - core if other else core) * columns, columns), columns)
    for r in range(begin, end, CHUNK):
        rows = pl.ds(r, CHUNK)
        out_ref[r - begin : r - begin + CHUNK, :] = sum(
            dot_nt(gp[i, rows, :], x_ref[i, own, k * n : (k + 1) * n]) for i in range(m) for k, gp in enumerate(gps)
        )
    if len(rest) > 1:
        out_ref[end - begin :, :] = rest[0][:, own]


def weight_half(gps, state, other, begin, end, *small):
    m, d, g = state.shape
    rows = end - begin + sum(one.shape[0] for one in small)
    return pl.pallas_call(
        functools.partial(weight_kernel, other, begin, end),
        in_specs=[VMEM] * (HALVES + 1 + len(small)),
        out_specs=VMEM,
        out_shape=jax.ShapeDtypeStruct((rows, d // 2), F32),
        compiler_params=params(16),
        cost_estimate=cost(m * (end - begin) * d * g, m * g * (2 * (end - begin) + d) + 2 * rows * d),
    )(*gps, state, *small)


def blocks_kernel(mine_ref, low_ref, high_ref, small_ref, out_ref):
    core = lax.rem(lax.axis_index("ens"), 2)
    h, columns = mine_ref.shape
    own = pl.ds(pl.multiple_of(core * columns, columns), columns)

    def fill(order):
        for place, block in enumerate(order):
            k, j = divmod(place, 8)
            rows = slice(16 * block, 16 * block + 16)
            got_ref, start = (low_ref, 0) if 16 * block < h // 2 else (high_ref, h // 2)
            got = got_ref[16 * block - start : 16 * block - start + 16, :]
            out_ref[k, 16 * j : 16 * j + 16, :] = mine_ref[rows, :] + got

    pl.when(core == 0)(lambda: fill(ORDER[0]))
    pl.when(core != 0)(lambda: fill(ORDER[1]))
    for k in range(8):
        rows = slice(16 * k, 16 * k + 16)
        out_ref[k, 128:, :] = small_ref[rows, own] + high_ref[h // 2 + 16 * k : h // 2 + 16 * k + 16, :]


def make_blocks(mine, low, high, small):
    return pl.pallas_call(
        blocks_kernel,
        in_specs=[VMEM] * 4,
        out_specs=VMEM,
        out_shape=jax.ShapeDtypeStruct((8, 144, 512), F32),
        compiler_params=params(16),
        cost_estimate=cost(1 << 19, 7 << 20),
        name="blocks",
    )(mine, low, high, small)


def gather_kernel(second_ref, out_ref, kept_ref):
    total = second_ref[0]
    for k in range(1, second_ref.shape[0]):
        total = total + second_ref[k]
    kept_ref[...] = total[:32]
    for k in range(out_ref.shape[0]):
        out_ref[k, :16, :] = total[32:]
        out_ref[k, 16:, :] = total[:16]


def gather_blocks(second):
    return pl.pallas_call(
        gather_kernel,
        in_specs=[VMEM],
        out_specs=[VMEM] * 2,
        out_shape=[jax.ShapeDtypeStruct((8, 32, 512), F32), jax.ShapeDtypeStruct((32, 512), F32)],
        compiler_params=params(16),
        name="gather",
    )(second)


def pick_kernel(kept_ref, third_ref, out_ref):
    core = lax.rem(lax.axis_index("ens"), 2)
    x = lax.rem(lax.axis_index("grid"), 4)
    y = lax.rem(lax.div(lax.axis_index("grid"), 4), 4)
    place = 2 * (2 * lax.div(x, 2) + lax.div(y, 2))

    @pl.when(core == 0)
    def _():
        out_ref[:32, :] = kept_ref[...]

    @pl.when(core != 0)
    def _():
        out_ref[:16, :] = third_ref[place, 16:, :]
        out_ref[16:32, :] = third_ref[place + 1, 16:, :]

    for k in range(third_ref.shape[0]):
        out_ref[32 + 16 * k : 48 + 16 * k, :] = third_ref[k, :16, :]


def pick(kept, third):
    return pl.pallas_call(
        pick_kernel,
        in_specs=[VMEM] * 2,
        out_specs=VMEM,
        out_shape=jax.ShapeDtypeStruct((160, 512), F32),
        compiler_params=params(16),
        name="pick",
    )(kept, third)


def finish_kernel(scale, done_ref, other_ref, in_ref, out_ref, bias_ref):
    core = lax.rem(lax.axis_index("ens"), 2)
    columns = done_ref.shape[1]
    for which, ref in ((core, done_ref), (1 - core, other_ref)):
        lanes = pl.ds(pl.multiple_of(columns * which, columns), columns)
        in_ref[:, lanes] = ref[:32, :] * scale
        out_ref[:, lanes] = ref[32:112, :] * scale
        bias_ref[:, lanes] = ref[112:113, :] * scale


def finish(scale, *operands):
    return pl.pallas_call(
        functools.partial(finish_kernel, scale),
        in_specs=[VMEM] * len(operands),
        out_specs=[VMEM] * 3,
        out_shape=[jax.ShapeDtypeStruct(shape, F32) for shape in ((32, 1024), (80, 1024), (1, 1024))],
        compiler_params=params(16),
        name="finish",
    )(*operands)


def latent_kernel(w_ref, *refs):
    gps, out_ref = refs[:HALVES], refs[HALVES]
    n = gps[0].shape[2]
    for k, gp in enumerate(gps):
        out_ref[0, :, k * n : (k + 1) * n] = dot(w_ref[...], gp[0]).astype(BF16)


def latent(wt, gps):
    m, h, n = gps[0].shape
    d = wt.shape[0]
    return pl.pallas_call(
        latent_kernel,
        grid=(m, d // CHUNK),
        in_specs=[pl.BlockSpec((CHUNK, h), lambda i, j: (j, 0))]
        + [pl.BlockSpec((1, h, n), lambda i, j: (i, 0, 0))] * HALVES,
        out_specs=pl.BlockSpec((1, CHUNK, HALVES * n), lambda i, j: (i, j, 0)),
        out_shape=jax.ShapeDtypeStruct((m, d, HALVES * n), BF16),
        compiler_params=params(),
        cost_estimate=cost(2 * m * h * d * n * HALVES, 2 * m * n * HALVES * (h + d)),
        name="latent",
    )(wt, *gps)


def shards(encoded_state, observed_state, location_importance, w_in, b_in, final_matrix):
    members = encoded_state.shape[0] * lax.axis_size("ens")
    points = encoded_state.shape[2] * lax.axis_size("grid")
    bias = b_in.reshape(-1, 128)
    location = location_importance.reshape(1, -1)
    factor = (1.0 - (1.0 - fair_alpha) / members) / (members - 1)

    hiddens, slopes, fcs = [], [], []
    weight = w_in
    for half in range(HALVES):
        hidden, slope, fc, *kept = forward(encoded_state, weight, bias, final_matrix, half, half == 0)
        if kept:
            weight, bias = kept
        hiddens.append(hidden)
        slopes.append(slope)
        across = lax.ppermute(fc, AXES, SWAP_Z)
        fcs.append((fc, across, lax.ppermute(fc, AXES, SWAP_CORE)))
    gps, init = [], ()
    for half in range(HALVES):
        fc, across, beside = fcs[half]
        if gps:
            across, gps[-1] = lax.optimization_barrier((across, gps[-1]))
        else:
            across, hiddens[-1] = lax.optimization_barrier((across, hiddens[-1]))
        diagonal = lax.ppermute(across, AXES, SWAP_CORE)
        everyone = (fc, beside, across, diagonal)
        gp, small = backward(
            everyone, observed_state, location, final_matrix, slopes[half], hiddens[half], init, factor, half
        )
        init = (small,)
        gps.append(gp)
    units = w_in.shape[0]
    low = weight_half(gps, encoded_state, True, 0, units // 2)
    low = lax.ppermute(low, AXES, SWAP_CORE)
    high = weight_half(gps, encoded_state, True, units // 2, units, small)
    high = lax.ppermute(high, AXES, SWAP_CORE)
    own = weight_half(gps, encoded_state, False, 0, units)
    blocks = make_blocks(own, low, high, small)
    blocks, late_weight = lax.optimization_barrier((blocks, w_in))
    first = all_to_all(blocks, CUBES[0])
    first, latent_sensitivity = lax.optimization_barrier((first, latent(late_weight.T, gps)))

    core = lax.axis_index("ens") % 2
    first = jnp.sum(first, 0)
    rows, small = first[:128], first[128:]
    split = jnp.broadcast_to(rows.reshape(8, 1, 16, 512), (8, 2, 16, 512)).reshape(8, 32, 512)
    whole = jnp.broadcast_to(rows.reshape(4, 1, 32, 512), (4, 2, 32, 512)).reshape(8, 32, 512)
    send = jnp.concatenate(
        [jnp.where(core == 1, split, whole), jnp.broadcast_to(small[None], (8, 16, 512))], 1
    )
    send, kept = gather_blocks(all_to_all(send, CUBES[1]))
    done = pick(kept, all_to_all(send, CUBES[0]))
    other = lax.ppermute(done, AXES, SWAP_CORE)
    in_sum, out_sum, bias_sum = finish(1.0 / math.sqrt(members * points), done, other)
    return latent_sensitivity, in_sum, out_sum, bias_sum.reshape(-1)


def solution(mesh):
    placed = (P("ens", None, "grid"), P(None, "grid"), P("grid"), P(), P(), P())
    return jax.shard_map(
        shards,
        mesh=mesh,
        in_specs=placed,
        out_specs=(P("ens", None, "grid"), P("grid", None), P(), P()),
        check_vma=False,
    )
```
